768 devices in a mesh: energy: 32 (over y, x_lo, core), space: 24 (over z, x_hi).
Axes of the slice: x: 4 (x_hi: 2, x_lo: 2; x = x_hi * 2 + x_lo), y: 8, z: 12, core: 2. Of those that a mesh axis runs over, the one named last changes fastest.
Arguments:
- greens: bfloat16 [2, 2, 32, 3072, 128], P(None, None, 'energy', 'space'), may hold values from -6 to 6
- coulomb: bfloat16 [3, 3072, 128], P(None, 'space'), may hold values from -0.3125 to 0.3125
- pattern: int32 [24, 2], P('space'), may hold values 0 or 1
Outputs:
- polar_sides: bfloat16 [2, 2, 2, 32, 3072, 128], P(None, None, None, 'energy', 'space')
- screened: bfloat16 [2, 2, 32, 3072, 128], P(None, None, 'energy', 'space')
The draws below stay inside these ranges and needn't reach their ends.
Inputs may be any that keep to these rules, and one draw needn't show every extreme that they name: pattern holds only 0 and 1.
All inputs are finite; a program needn't handle non-finite values. No bound on the sum of `pattern` on one device may be relied on, other than what follows from the above.
Results may differ from the reference program's by a relative error of at most 0.0077.
Values may be sent and summed in bfloat16 or wider, within the bound.
A program may use at most 32 MiB of HBM per device.

```python
import math
import jax
import jax.numpy as jnp
from jax import lax

BS = 128
NE = 32
PERIOD = 64
NB = 24


def plant(values, rng, smallest, largest):
    spot = [jax.random.randint(jax.random.fold_in(rng, axis), (), 0, length) for axis, length in enumerate(values.shape)]
    main_axis = values.shape.index(max(values.shape))
    neighbour = spot[:main_axis] + [(spot[main_axis] + 1) % values.shape[main_axis]] + spot[main_axis + 1:]
    return values.at[tuple(spot)].set(smallest).at[tuple(neighbour)].set(largest)


def level_of(own_key, dims, shards, least, largest):
    def one(axis_at, blocks):
        draws = jax.random.uniform(jax.random.fold_in(jax.random.fold_in(own_key, 6), axis_at), (blocks,), jnp.float32, least / len(shards), largest / len(shards))
        return jnp.repeat(jnp.exp(draws), dims[axis_at] // blocks).reshape((-1,) + (1,) * (len(dims) - axis_at - 1))

    gain = one(*shards[0])
    for cut in shards[1:]:
        gain = gain * one(*cut)
    return gain


def scatter_about(key, shape, scale, limit, cuts=(), kind=jnp.bfloat16):
    drawn = jax.random.normal(key, shape, jnp.float32) * scale
    if len(cuts) > 0:
        drawn = level_of(key, shape, cuts, -0.22, 0.18) * drawn
    return jnp.clip(drawn, min=-limit, max=limit).astype(kind)


def setup_inputs(seed: int = 0) -> dict:
    key_list = jax.random.split(jax.random.key(seed), 4)
    greens = scatter_about(key_list[0], (2, 2, NE, NB * BS, BS), 1.0, 6.0, ((2, 32), (3, 24)))
    coulomb = scatter_about(key_list[1], (3, NB * BS, BS), (3 * BS) ** -0.5, 0.3125, ((1, 24),))
    pattern = plant((jax.random.randint(key_list[2], (NB, 2), 0, 4) < 3).astype(jnp.int32), jax.random.fold_in(key_list[2], 1), 0, 1)
    return {"greens": greens, "coulomb": coulomb, "pattern": pattern}


def make_tables(energies):
    period = 2 * energies
    times = jnp.arange(period, dtype=jnp.int32)
    levels = jnp.arange(energies, dtype=jnp.int32)
    phases = (times[:, None] * levels[None, :] % period).astype(jnp.float32) * jnp.float32(2.0 * math.pi / period)
    cos_part = jnp.cos(phases)
    sin_part = jnp.sin(phases)
    forward_table = jnp.concatenate([jnp.concatenate([cos_part, sin_part], axis=1), jnp.concatenate([-sin_part, cos_part], axis=1)], axis=0).astype(jnp.bfloat16)
    cos_back = cos_part.T
    sin_back = sin_part.T
    factor = 1.0 / (period * math.sqrt(energies))
    rows_list = [jnp.concatenate([cos_back, -sin_back], axis=1), jnp.concatenate([sin_back, cos_back], axis=1), jnp.concatenate([-cos_back, -sin_back], axis=1), jnp.concatenate([-sin_back, cos_back], axis=1)]
    inverse_table = (jnp.concatenate(rows_list, axis=0) * jnp.float32(factor)).astype(jnp.bfloat16)
    return (forward_table, inverse_table)

def time_product(time_fields, period):
    less_re = time_fields[0, :period]
    less_im = time_fields[0, period:]
    great_re = time_fields[1, :period]
    great_im = time_fields[1, period:]
    real_part = less_re * great_im - less_im * great_re
    imag_part = less_re * great_re + less_im * great_im
    return jnp.concatenate([real_part, imag_part], axis=0).astype(jnp.bfloat16)

def project(coupling, spectra):
    return jnp.einsum('rc,xcd->xrd', coupling.astype(jnp.float32), spectra.astype(jnp.float32)).astype(jnp.bfloat16)

def closing(image, coupling):
    return jnp.einsum('xrc,sc->xrs', image.astype(jnp.float32), coupling.astype(jnp.float32))

def reference(greens, coulomb, pattern):
    forward_table, inverse_table = make_tables(NE)

    def polar_row(block_rows):
        stacked = block_rows.reshape(2, 2 * NE, BS * BS)
        time_fields = jnp.einsum('tk,akn->atn', forward_table.astype(jnp.float32), stacked.astype(jnp.float32))
        product = time_product(time_fields, PERIOD)
        spectra = jnp.dot(inverse_table, product, preferred_element_type=jnp.float32).astype(jnp.bfloat16)
        return spectra.reshape(4 * NE, BS, BS)

    def coulomb_row(inputs):
        below_block, own_block, above_block, couplings, pattern_row = inputs
        link_marks = pattern_row.astype(jnp.bfloat16)
        lower_coupling = couplings[0] * link_marks[0]
        diag_coupling = couplings[1]
        upper_coupling = couplings[2] * link_marks[1]
        side_lower = project(lower_coupling, below_block)
        side_upper = project(upper_coupling, above_block)
        own_image = project(diag_coupling, own_block)
        summed = closing(side_lower, lower_coupling) + closing(own_image, diag_coupling) + closing(side_upper, upper_coupling)
        return (jnp.stack([side_lower, side_upper], axis=0), summed.astype(jnp.bfloat16))
    rows_first = jnp.moveaxis(greens.reshape(2, 2, NE, NB, BS, BS), 3, 0)
    polar = lax.map(polar_row, rows_first)
    zeros_block = jnp.zeros((1, 4 * NE, BS, BS), jnp.bfloat16)
    padded = jnp.concatenate([zeros_block, polar, zeros_block], axis=0)
    couplings = jnp.transpose(coulomb.reshape(3, NB, BS, BS), (1, 0, 2, 3))
    sides, summed = lax.map(coulomb_row, (padded[:-2], polar, padded[2:], couplings, pattern))
    sides = sides.reshape(NB, 2, 2, 2, NE, BS, BS)
    sides = jnp.transpose(sides, (2, 1, 3, 4, 0, 5, 6)).reshape(2, 2, 2, NE, NB * BS, BS)
    summed = summed.reshape(NB, 2, 2, NE, BS, BS)
    summed = jnp.transpose(summed, (1, 2, 3, 0, 4, 5)).reshape(2, 2, NE, NB * BS, BS)
    return (sides, summed)
```

```python
import math

import jax
import jax.numpy as jnp
import numpy as np
from jax import lax
from jax.experimental import pallas as pl
from jax.experimental.pallas import tpu as pltpu
from jax.sharding import PartitionSpec as P

MESH = pl.DeviceIdType.MESH
BF16 = jnp.bfloat16


def make_tables(energies, rows):
    period = 2 * energies
    phases = (np.arange(period)[:, None] * np.arange(energies)[None, :] % period) * (2.0 * math.pi / period)
    cos_part, sin_part = np.cos(phases), np.sin(phases)
    forward = np.block([[cos_part, sin_part], [-sin_part, cos_part]])
    cos_back, sin_back = cos_part.T, sin_part.T
    inverse = np.block(
        [[cos_back, -sin_back], [sin_back, cos_back], [-cos_back, -sin_back], [-sin_back, cos_back]]
    ) * (1.0 / (period * math.sqrt(energies)))
    unit = np.eye(rows)
    return tuple(np.kron(table, unit).astype(np.float32).astype(BF16) for table in (forward, inverse))


def kernel(
    n_energy, n_space,
    greens, coulomb, pattern, forward, inverse,
    sides, screened,
    own, gathered, spectra, polar, fwd, inv, coul,
    send_sem, gather_sem, return_sem, side_send, side_sem, local_sem,
):
    e = lax.axis_index("energy")
    s = lax.axis_index("space")
    size = own.shape[1]
    rows = size // n_energy
    above = lax.rem(s + 1, n_space)
    below = lax.rem(s + n_space - 1, n_space)

    def peer(k):
        return lax.rem(e + k, n_energy)

    def part(ref, index):
        return ref.at[:, pl.ds(pl.multiple_of(index * rows, rows), rows), :]

    loads = [
        pltpu.make_async_copy(greens, own, local_sem.at[0]),
        pltpu.make_async_copy(forward, fwd, local_sem.at[1]),
        pltpu.make_async_copy(inverse, inv, local_sem.at[2]),
        pltpu.make_async_copy(coulomb, coul, local_sem.at[3]),
    ]
    for load in loads:
        load.start()

    barrier = pltpu.get_barrier_semaphore()

    def greet(k, carry):
        pl.semaphore_signal(barrier, inc=1, device_id={"energy": peer(k)}, device_id_type=MESH)
        return carry

    lax.fori_loop(1, n_energy, greet, 0)
    for other in (above, below):
        pl.semaphore_signal(barrier, inc=1, device_id={"space": other}, device_id_type=MESH)
    pl.semaphore_wait(barrier, n_energy + 1)
    loads[0].wait()

    def exchange(source, target, send, recv):
        def step(k, carry):
            to = peer(k)
            pltpu.make_async_remote_copy(
                src_ref=part(source, to),
                dst_ref=part(target, e),
                send_sem=send,
                recv_sem=recv,
                device_id={"energy": to},
                device_id_type=MESH,
            ).start()
            return carry

        lax.fori_loop(1, n_energy, step, 0)
        mine = pltpu.make_async_copy(part(source, e), part(target, e), local_sem.at[0])
        mine.start()
        mine.wait()

    def settle(ref, sem):
        whole = ref.at[:, pl.ds(0, size - rows), :]
        pltpu.make_async_copy(whole, whole, sem).wait()

    exchange(own, gathered, send_sem.at[0], gather_sem)
    loads[1].wait()
    loads[2].wait()
    settle(gathered, gather_sem)

    half = 2 * size
    stacked = jnp.concatenate(
        [gathered[0:2].reshape(half, size), gathered[2:4].reshape(half, size)], axis=1
    )
    fields = jnp.dot(fwd[...], stacked, preferred_element_type=jnp.float32)
    less_re, less_im = fields[:half, :size], fields[half:, :size]
    great_re, great_im = fields[:half, size:], fields[half:, size:]
    product = jnp.concatenate(
        [less_re * great_im - less_im * great_re, less_re * great_re + less_im * great_im], axis=0
    ).astype(BF16)
    spectra[...] = (
        jnp.dot(inv[...], product, preferred_element_type=jnp.float32).astype(BF16).reshape(4, size, size)
    )

    exchange(spectra, polar.at[0], send_sem.at[1], return_sem)
    settle(polar.at[0], return_sem)

    hops = []
    for slot, other in ((1, above), (2, below)):
        hop = pltpu.make_async_remote_copy(
            src_ref=polar.at[0],
            dst_ref=polar.at[slot],
            send_sem=side_send.at[slot - 1],
            recv_sem=side_sem.at[slot - 1],
            device_id={"space": other},
            device_id_type=MESH,
        )
        hop.start()
        hops.append(hop)

    loads[3].wait()
    has_below = jnp.where(s > 0, pattern[0, 0], 0).astype(jnp.float32)
    has_above = jnp.where(s < n_space - 1, pattern[0, 1], 0).astype(jnp.float32)
    lower = (coul[0].astype(jnp.float32) * has_below).astype(BF16)
    upper = (coul[2].astype(jnp.float32) * has_above).astype(BF16)
    couplings = (coul[1], lower, upper)

    def images(slot):
        wide = jnp.concatenate([polar[slot, i] for i in range(4)], axis=1)
        return jnp.dot(couplings[slot], wide, preferred_element_type=jnp.float32).astype(BF16)

    own_image = images(0)
    for hop in hops:
        hop.wait_recv()
    side_lower = images(1)
    side_upper = images(2)
    weights = jnp.concatenate([lower, coul[1], upper], axis=1)
    for kind in range(2):
        for portion in range(2):
            i = 2 * kind + portion
            cut = slice(i * size, (i + 1) * size)
            sides[kind, 0, portion, 0] = side_lower[:, cut]
            sides[kind, 1, portion, 0] = side_upper[:, cut]
            joined = jnp.concatenate([side_lower[:, cut], own_image[:, cut], side_upper[:, cut]], axis=1)
            screened[kind, portion, 0] = lax.dot_general(
                joined, weights, (((1,), (1,)), ((), ())), preferred_element_type=jnp.float32
            ).astype(BF16)

    settle(own, send_sem.at[0])
    settle(spectra, send_sem.at[1])
    for hop in hops:
        hop.wait_send()


def solution(mesh):
    n_energy, n_space = mesh.shape["energy"], mesh.shape["space"]

    def local(greens, coulomb, pattern):
        size = greens.shape[-1]
        rows = size // n_energy
        forward, inverse = make_tables(n_energy, rows)
        blocks = pltpu.VMEM((4, size, size), BF16)
        anywhere = pl.BlockSpec(memory_space=pl.ANY)
        vmem = pl.BlockSpec(memory_space=pltpu.VMEM)
        return pl.pallas_call(
            lambda *refs: kernel(n_energy, n_space, *refs),
            out_shape=(
                jax.ShapeDtypeStruct((2, 2, 2, 1, size, size), BF16),
                jax.ShapeDtypeStruct((2, 2, 1, size, size), BF16),
            ),
            in_specs=[anywhere, anywhere, pl.BlockSpec(memory_space=pltpu.SMEM), anywhere, anywhere],
            out_specs=(vmem, vmem),
            scratch_shapes=[
                blocks, blocks, blocks,
                pltpu.VMEM((3, 4, size, size), BF16),
                pltpu.VMEM(forward.shape, BF16),
                pltpu.VMEM(inverse.shape, BF16),
                pltpu.VMEM((3, size, size), BF16),
                pltpu.SemaphoreType.DMA((2,)),
                pltpu.SemaphoreType.DMA,
                pltpu.SemaphoreType.DMA,
                pltpu.SemaphoreType.DMA((2,)),
                pltpu.SemaphoreType.DMA((2,)),
                pltpu.SemaphoreType.DMA((4,)),
            ],
            compiler_params=pltpu.CompilerParams(collective_id=0, has_side_effects=True),
            name="polarization",
        )(greens.reshape(4, size, size), coulomb.reshape(3, size, size), pattern, jnp.asarray(forward), jnp.asarray(inverse))

    return jax.shard_map(
        local,
        mesh=mesh,
        in_specs=(P(None, None, "energy", "space", None), P(None, "space", None), P("space", None)),
        out_specs=(P(None, None, None, "energy", "space", None), P(None, None, "energy", "space", None)),
        check_vma=False,
    )
```

```python
import math

import jax
import jax.numpy as jnp
import numpy as np
from jax import lax
from jax.experimental import pallas as pl
from jax.experimental.pallas import tpu as pltpu
from jax.sharding import PartitionSpec as P

MESH = pl.DeviceIdType.MESH
BF16 = jnp.bfloat16


def make_tables(energies, rows):
    period = 2 * energies
    phases = (np.arange(period)[:, None] * np.arange(energies)[None, :] % period) * (2.0 * math.pi / period)
    cos_part, sin_part = np.cos(phases), np.sin(phases)
    forward = np.block([[cos_part, sin_part], [-sin_part, cos_part]])
    cos_back, sin_back = cos_part.T, sin_part.T
    inverse = np.block(
        [[cos_back, -sin_back], [sin_back, cos_back], [-cos_back, -sin_back], [-sin_back, cos_back]]
    ) * (1.0 / (period * math.sqrt(energies)))
    unit = np.eye(rows)
    return tuple(np.kron(table, unit).astype(np.float32).astype(BF16) for table in (forward, inverse))


def exchange_kernel(
    n_energy, n_space, rows,
    greens, forward, inverse,
    polar,
    gathered, spectra, fwd, inv,
    gather_send, gather_sem, return_send, return_sem, x_send, x_sem, z_send, z_sem, local_sem,
):
    e = lax.axis_index("energy")
    s = lax.axis_index("space")
    n_y = n_energy // 4
    core, x, y = e % 2, (e // 2) % 2, e // 4
    high, z = s % 2, s // 2
    n_z = n_space // 2
    mine = e // 2
    partner = s + 1 - 2 * high
    z_to, z_from = s + 2 - 4 * high, s - 2 + 4 * high
    relays = jnp.where(high == 0, z < n_z - 1, z > 0)
    receives = jnp.where(high == 0, z > 0, z < n_z - 1)
    distances = [n_y // 2]
    for d in range(n_y // 2 - 1, 0, -1):
        distances += [d, -d]

    def part(ref, index):
        return ref.at[:, :, pl.ds(pl.multiple_of(index * rows, rows), rows), :]

    def strip(ref, y_from):
        return ref.at[:, :, pl.ds(pl.multiple_of(y_from * 2 * rows, 2 * rows), 2 * rows), :]

    def at_distance(d):
        return (y + d + n_y) % n_y

    @pl.when(core == 1)
    def _():
        pltpu.make_async_copy(forward, fwd, local_sem.at[0]).start()
        pltpu.make_async_copy(inverse, inv, local_sem.at[1]).start()

    barrier = pltpu.get_barrier_semaphore()
    pl.semaphore_signal(barrier, inc=1, device_id={"space": partner}, device_id_type=MESH)

    @pl.when(receives)
    def _():
        pl.semaphore_signal(barrier, inc=1, device_id={"space": z_from}, device_id_type=MESH)

    @pl.when(core == 1)
    def _():
        def greet(k, carry):
            pl.semaphore_signal(barrier, inc=1, device_id={"energy": (e + k) % n_energy}, device_id_type=MESH)
            return carry

        lax.fori_loop(1, n_energy, greet, 0)

    pl.semaphore_wait(barrier, n_energy // 2 + 1 - core + jnp.where(relays, 1, 0))

    def give(to):
        pltpu.make_async_remote_copy(
            src_ref=part(greens, to),
            dst_ref=part(gathered, e),
            send_sem=gather_send,
            recv_sem=gather_sem,
            device_id={"energy": 2 * to + 1},
            device_id_type=MESH,
        ).start()

    for d in distances:
        for across in (1, 0):
            give(2 * at_distance(d) + (x + across) % 2)
    give(2 * y + 1 - x)

    @pl.when(core == 0)
    def _():
        give(mine)

    @pl.when(jnp.logical_not(receives))
    def _():
        polar[2] = jnp.zeros(polar.shape[1:], BF16)

    @pl.when(core == 1)
    def _():
        own = pltpu.make_async_copy(part(greens, mine), part(gathered, e), local_sem.at[2])
        own.start()
        pltpu.make_async_copy(forward, fwd, local_sem.at[0]).wait()
        pltpu.make_async_copy(inverse, inv, local_sem.at[1]).wait()
        own.wait()
        others = gathered.at[:, :, pl.ds(0, (n_energy - 1) * rows), :]
        pltpu.make_async_copy(others, others, gather_sem).wait()

        size = gathered.shape[-1]
        half = 2 * size
        stacked = jnp.concatenate(
            [
                jnp.concatenate([gathered[2 * a, h], gathered[2 * a + 1, h]], axis=0)
                for a in range(2)
                for h in range(2)
            ],
            axis=1,
        )
        fields = jnp.dot(fwd[...], stacked, preferred_element_type=jnp.float32)
        less_re, less_im = fields[:half, :half], fields[half:, :half]
        great_re, great_im = fields[:half, half:], fields[half:, half:]
        product = jnp.concatenate(
            [less_re * great_im - less_im * great_re, less_re * great_re + less_im * great_im], axis=0
        ).astype(BF16)
        result = jnp.dot(inv[...], product, preferred_element_type=jnp.float32).astype(BF16)
        for i in range(4):
            for h in range(2):
                spectra[i, h] = result[i * size:(i + 1) * size, h * size:(h + 1) * size]

        def give_back(to):
            pltpu.make_async_remote_copy(
                src_ref=part(spectra, to),
                dst_ref=part(polar.at[0], mine),
                send_sem=return_send,
                recv_sem=return_sem.at[y],
                device_id={"energy": to},
                device_id_type=MESH,
            ).start()

        for d in distances:
            for across in (1, 0):
                for c in (0, 1):
                    give_back(4 * at_distance(d) + 2 * ((x + across) % 2) + c)
        for c in (0, 1):
            give_back(4 * y + 2 * (1 - x) + c)
        give_back(e - 1)
        keep = pltpu.make_async_copy(part(spectra, e), part(polar.at[0], mine), local_sem.at[2])
        keep.start()
        keep.wait()

    def hop(y_from):
        return pltpu.make_async_remote_copy(
            src_ref=strip(polar.at[0], y_from),
            dst_ref=strip(polar.at[1], y_from),
            send_sem=x_send,
            recv_sem=x_sem.at[y_from],
            device_id={"space": partner},
            device_id_type=MESH,
        )

    def relay(y_from):
        return pltpu.make_async_remote_copy(
            src_ref=strip(polar.at[1], y_from),
            dst_ref=strip(polar.at[2], y_from),
            send_sem=z_send,
            recv_sem=z_sem.at[y_from],
            device_id={"space": z_to},
            device_id_type=MESH,
        )

    order = [y] + [at_distance(d) for d in distances[::-1]]
    one = part(polar.at[0], 0)
    for y_from in order:
        landed = strip(polar.at[0], y_from)
        if y_from is y:
            @pl.when(core == 0)
            def _():
                pltpu.make_async_copy(landed, landed, return_sem.at[y]).wait()

            @pl.when(core == 1)
            def _():
                pltpu.make_async_copy(one, one, return_sem.at[y]).wait()
        else:
            pltpu.make_async_copy(landed, landed, return_sem.at[y_from]).wait()
        hop(y_from).start()

    for y_from in order:
        hop(y_from).wait_recv()

        @pl.when(relays)
        def _():
            relay(y_from).start()

    @pl.when(receives)
    def _():
        for y_from in order:
            relay(y_from).wait_recv()

    sent = gathered.at[:, :, pl.ds(0, (n_energy // 2 - 1) * rows), :]
    pltpu.make_async_copy(sent, sent, gather_send).wait()

    @pl.when(core == 0)
    def _():
        pltpu.make_async_copy(one, one, gather_send).wait()

    @pl.when(core == 1)
    def _():
        back = spectra.at[:, :, pl.ds(0, (n_energy - 1) * rows), :]
        pltpu.make_async_copy(back, back, return_send).wait()

    pltpu.make_async_copy(polar.at[0], polar.at[0], x_send).wait()

    @pl.when(relays)
    def _():
        pltpu.make_async_copy(polar.at[0], polar.at[0], z_send).wait()


def product_kernel(n_space, polar, coulomb, pattern, sides, screened, out_sides, out_screened, out_sem):
    size = coulomb.shape[-1]
    s = lax.axis_index("space")
    high = s % 2

    def coupling(upper):
        present = jnp.where(jnp.where(upper == 1, s < n_space - 1, s > 0), pattern[0, upper], 0)
        return (coulomb[2 * upper].astype(jnp.float32) * present.astype(jnp.float32)).astype(BF16)

    def image(weight, slot):
        wide = jnp.concatenate([polar[slot, i].reshape(size, size) for i in range(4)], axis=1)
        return jnp.dot(weight, wide, preferred_element_type=jnp.float32).astype(BF16)

    weights = (coulomb[1], coupling(1 - high), coupling(high))
    images = [image(weight, slot) for slot, weight in enumerate(weights)]
    copies = []
    for slot, block in ((1, 1 - high), (2, high)):
        for i in range(4):
            out_sides[slot - 1, i] = images[slot][:, i * size:(i + 1) * size]
        for kind in range(2):
            copies.append(
                pltpu.make_async_copy(
                    out_sides.at[slot - 1, pl.ds(2 * kind, 2)], sides.at[kind, block], out_sem.at[len(copies)]
                )
            )
            copies[-1].start()
    joined_weights = jnp.concatenate(weights, axis=1)
    for i in range(4):
        joined = jnp.concatenate([part[:, i * size:(i + 1) * size] for part in images], axis=1)
        out_screened[i] = lax.dot_general(
            joined, joined_weights, (((1,), (1,)), ((), ())), preferred_element_type=jnp.float32
        ).astype(BF16)
    copies.append(pltpu.make_async_copy(out_screened, screened, out_sem.at[len(copies)]))
    copies[-1].start()
    for copy in copies:
        copy.wait()


def solution(mesh):
    n_energy, n_space = mesh.shape["energy"], mesh.shape["space"]

    def local(greens, coulomb, pattern):
        size = greens.shape[-1]
        rows = size // n_energy
        forward, inverse = make_tables(n_energy, rows)
        anywhere = pl.BlockSpec(memory_space=pl.ANY)
        vmem = pl.BlockSpec(memory_space=pltpu.VMEM)
        dma = pltpu.SemaphoreType.DMA
        strips = n_energy // 4
        polar = pl.pallas_call(
            lambda *refs: exchange_kernel(n_energy, n_space, rows, *refs),
            out_shape=pltpu.VMEM((3, 4, 2, size // 2, size), BF16),
            in_specs=[anywhere] * 3,
            out_specs=vmem,
            scratch_shapes=[
                pltpu.VMEM((4, 2, size, size), BF16),
                pltpu.VMEM((4, 2, size, size), BF16),
                pltpu.VMEM(forward.shape, BF16),
                pltpu.VMEM(inverse.shape, BF16),
                dma, dma, dma, dma((strips,)), dma, dma((strips,)), dma, dma((strips,)), dma((3,)),
            ],
            compiler_params=pltpu.CompilerParams(collective_id=0, has_side_effects=True),
            name="exchange",
        )(greens.reshape(4, 2, size // 2, size), jnp.asarray(forward), jnp.asarray(inverse))
        sides, screened = pl.pallas_call(
            lambda *refs: product_kernel(n_space, *refs),
            out_shape=(
                jax.ShapeDtypeStruct((2, 2, 2, size, size), BF16),
                jax.ShapeDtypeStruct((4, size, size), BF16),
            ),
            in_specs=[vmem, vmem, pl.BlockSpec(memory_space=pltpu.SMEM)],
            out_specs=(anywhere, anywhere),
            scratch_shapes=[
                pltpu.VMEM((2, 4, size, size), BF16),
                pltpu.VMEM((4, size, size), BF16),
                dma((5,)),
            ],
            compiler_params=pltpu.CompilerParams(vmem_limit_bytes=16 << 20),
            name="products",
        )(polar, coulomb.reshape(3, size, size), pattern)
        return sides.reshape(2, 2, 2, 1, size, size), screened.reshape(2, 2, 1, size, size)

    return jax.shard_map(
        local,
        mesh=mesh,
        in_specs=(P(None, None, "energy", "space", None), P(None, "space", None), P("space", None)),
        out_specs=(P(None, None, None, "energy", "space", None), P(None, None, "energy", "space", None)),
        check_vma=False,
    )
```

```python
import math

import jax
import jax.numpy as jnp
import numpy as np
from jax import lax
from jax.experimental import pallas as pl
from jax.experimental.pallas import tpu as pltpu
from jax.sharding import PartitionSpec as P

MESH = pl.DeviceIdType.MESH
BF16 = jnp.bfloat16
DIRECT = 5


def make_tables(energies, rows):
    period = 2 * energies
    phases = (np.arange(period)[:, None] * np.arange(energies)[None, :] % period) * (2.0 * math.pi / period)
    cos_part, sin_part = np.cos(phases), np.sin(phases)
    forward = np.block([[cos_part, sin_part], [-sin_part, cos_part]])
    cos_back, sin_back = cos_part.T, sin_part.T
    inverse = np.block(
        [[cos_back, -sin_back], [sin_back, cos_back], [-cos_back, -sin_back], [-sin_back, cos_back]]
    ) * (1.0 / (period * math.sqrt(energies)))
    unit = np.eye(rows)
    return tuple(np.kron(table, unit).astype(np.float32).astype(BF16) for table in (forward, inverse))


def exchange_kernel(
    n_energy, n_space, rows,
    greens, forward, inverse,
    polar,
    gathered, spectra, staged, fwd, inv,
    gather_send, gather_sem, stage_send, stage_sem, own_send, own_sem, x_send, x_sem, z_send, z_sem, diag_send, local_sem,
):
    e = lax.axis_index("energy")
    s = lax.axis_index("space")
    n_y = n_energy // 4
    core, x, y = e % 2, (e // 2) % 2, e // 4
    high, z = s % 2, s // 2
    n_z = n_space // 2
    mine = e // 2
    partner = s + 1 - 2 * high
    z_to, z_from = s + 2 - 4 * high, s - 2 + 4 * high
    diagonal = s - 1 + 2 * high
    relays = jnp.where(high == 0, z < n_z - 1, z > 0)
    receives = jnp.where(high == 0, z > 0, z < n_z - 1)
    near = []
    for d in range(1, n_y // 2):
        near += [d, -d]
    near.append(n_y // 2)
    far = near[::-1]

    def part(ref, index):
        return ref.at[:, :, pl.ds(pl.multiple_of(index * rows, rows), rows), :]

    def strip(ref, y_from):
        return ref.at[:, :, pl.ds(pl.multiple_of(y_from * 2 * rows, 2 * rows), 2 * rows), :]

    def at_distance(d):
        return (y + d + n_y) % n_y

    def device(y_to, x_to, core_to):
        return 4 * y_to + 2 * x_to + core_to

    barrier = pltpu.get_barrier_semaphore()

    @pl.when(core == 1)
    def _():
        def greet(to):
            pl.semaphore_signal(barrier, inc=1, device_id={"energy": to}, device_id_type=MESH)

        for d in far:
            for x_to in range(2):
                for c in range(2):
                    greet(device(at_distance(d), x_to, c))
        greet(device(y, 1 - x, 0))
        greet(device(y, 1 - x, 1))
        greet(e - 1)

    for x_to in range(2):
        pl.semaphore_signal(
            barrier, inc=1, device_id={"energy": device(y, x_to, 1), "space": partner}, device_id_type=MESH
        )

    @pl.when(receives)
    def _():
        pl.semaphore_signal(barrier, inc=1, device_id={"space": z_from}, device_id_type=MESH)
        for x_to in range(2):
            pl.semaphore_signal(
                barrier, inc=1, device_id={"energy": device(y, x_to, 1), "space": diagonal}, device_id_type=MESH
            )

    @pl.when(core == 1)
    def _():
        pltpu.make_async_copy(forward, fwd, local_sem.at[0]).start()
        pltpu.make_async_copy(inverse, inv, local_sem.at[1]).start()

    pl.semaphore_wait(
        barrier,
        n_energy // 2 + 3 * core + jnp.where(relays, 1, 0) + jnp.where(receives, 4 * core, 0),
    )

    def give(to):
        pltpu.make_async_remote_copy(
            src_ref=part(greens, to),
            dst_ref=part(gathered, e),
            send_sem=gather_send,
            recv_sem=gather_sem,
            device_id={"energy": 2 * to + 1},
            device_id_type=MESH,
        ).start()

    for d in far:
        for across in (1, 0):
            give(2 * at_distance(d) + (x + across) % 2)
    give(2 * y + 1 - x)

    @pl.when(core == 0)
    def _():
        give(mine)

    @pl.when(jnp.logical_not(receives))
    def _():
        polar[2] = jnp.zeros(polar.shape[1:], BF16)

    def stage(y_from, y_to):
        block = 4 * rows
        return pltpu.make_async_remote_copy(
            src_ref=spectra.at[:, :, pl.ds(pl.multiple_of(y_to * block, block), block), :],
            dst_ref=staged.at[y_from],
            send_sem=stage_send,
            recv_sem=stage_sem.at[y_from],
            device_id={"energy": device(y_to, x, 1)},
            device_id_type=MESH,
        )

    def hand_out(y_from, piece, direct):
        index = 2 * y_from + x
        if direct:
            @pl.when(receives)
            def _():
                for x_to in range(2):
                    for c in range(2):
                        pltpu.make_async_remote_copy(
                            src_ref=piece(2 * x_to + c),
                            dst_ref=part(polar.at[2], index),
                            send_sem=diag_send,
                            recv_sem=z_sem.at[y_from],
                            device_id={"energy": device(y, x_to, c), "space": diagonal},
                            device_id_type=MESH,
                        ).start()

        for across in (0, 1):
            for c in (0, 1):
                x_to = (x + across) % 2
                pltpu.make_async_remote_copy(
                    src_ref=piece(2 * x_to + c),
                    dst_ref=part(polar.at[1], index),
                    send_sem=x_send,
                    recv_sem=x_sem.at[y_from],
                    device_id={"energy": device(y, x_to, c), "space": partner},
                    device_id_type=MESH,
                ).start()
        for across, c in ((1, 0), (1, 1), (0, 0)):
            x_to = (x + across) % 2
            pltpu.make_async_remote_copy(
                src_ref=piece(2 * x_to + c),
                dst_ref=part(polar.at[0], index),
                send_sem=own_send,
                recv_sem=own_sem,
                device_id={"energy": device(y, x_to, c)},
                device_id_type=MESH,
            ).start()
        pltpu.make_async_copy(piece(2 * x + 1), part(polar.at[0], index), local_sem.at[2]).start()

    @pl.when(core == 1)
    def _():
        own = pltpu.make_async_copy(part(greens, mine), part(gathered, e), local_sem.at[2])
        own.start()
        pltpu.make_async_copy(forward, fwd, local_sem.at[0]).wait()
        pltpu.make_async_copy(inverse, inv, local_sem.at[1]).wait()
        own.wait()
        others = gathered.at[:, :, pl.ds(0, (n_energy - 1) * rows), :]
        pltpu.make_async_copy(others, others, gather_sem).wait()

        size = gathered.shape[-1]
        half = 2 * size
        stacked = jnp.concatenate(
            [
                jnp.concatenate([gathered[2 * a, h], gathered[2 * a + 1, h]], axis=0)
                for a in range(2)
                for h in range(2)
            ],
            axis=1,
        )
        fields = jnp.dot(fwd[...], stacked, preferred_element_type=jnp.float32)
        less_re, less_im = fields[:half, :half], fields[half:, :half]
        great_re, great_im = fields[:half, half:], fields[half:, half:]
        product = jnp.concatenate(
            [less_re * great_im - less_im * great_re, less_re * great_re + less_im * great_im], axis=0
        ).astype(BF16)
        result = jnp.dot(inv[...], product, preferred_element_type=jnp.float32).astype(BF16)
        for i in range(4):
            for h in range(2):
                spectra[i, h] = result[i * size:(i + 1) * size, h * size:(h + 1) * size]

        for d in far:
            stage(y, at_distance(d)).start()
        hand_out(y, lambda j: part(spectra, 4 * y + j), False)
        for i, d in enumerate(near):
            y_from = at_distance(d)
            stage(y_from, y_from).wait_recv()
            hand_out(y_from, lambda j: staged.at[y_from, :, :, pl.ds(j * rows, rows), :], i >= n_y - 1 - DIRECT)

    def relay(y_from):
        return pltpu.make_async_remote_copy(
            src_ref=strip(polar.at[1], y_from),
            dst_ref=strip(polar.at[2], y_from),
            send_sem=z_send,
            recv_sem=z_sem.at[y_from],
            device_id={"space": z_to},
            device_id_type=MESH,
        )

    order = [y] + [at_distance(d) for d in near]
    for i, y_from in enumerate(order):
        landed = strip(polar.at[1], y_from)
        pltpu.make_async_copy(landed, landed, x_sem.at[y_from]).wait()
        if i < n_y - DIRECT:
            @pl.when(relays)
            def _():
                relay(y_from).start()

    half_own = polar.at[0, pl.ds(0, 2)]

    @pl.when(core == 0)
    def _():
        pltpu.make_async_copy(polar.at[0], polar.at[0], own_sem).wait()

    @pl.when(core == 1)
    def _():
        pltpu.make_async_copy(half_own, half_own, own_sem).wait()
        pltpu.make_async_copy(half_own, half_own, local_sem.at[2]).wait()

    sent = gathered.at[:, :, pl.ds(0, (n_energy // 2 - 1) * rows), :]
    pltpu.make_async_copy(sent, sent, gather_send).wait()

    @pl.when(core == 0)
    def _():
        one = part(polar.at[0], 0)
        pltpu.make_async_copy(one, one, gather_send).wait()

    @pl.when(core == 1)
    def _():
        back = spectra.at[:, :, pl.ds(0, (n_y - 1) * 4 * rows), :]
        pltpu.make_async_copy(back, back, stage_send).wait()
        six = staged.at[pl.ds(0, 6)]
        pltpu.make_async_copy(six, six, own_send).wait()
        two = polar.at[pl.ds(0, 2)]
        pltpu.make_async_copy(two, two, x_send).wait()

    @pl.when(relays)
    def _():
        relayed = polar.at[1, :, :, pl.ds(0, (n_y - DIRECT) * 2 * rows), :]
        pltpu.make_async_copy(relayed, relayed, z_send).wait()

    @pl.when(receives)
    def _():
        if DIRECT > 0:
            @pl.when(core == 1)
            def _():
                direct = staged.at[pl.ds(0, DIRECT)]
                pltpu.make_async_copy(direct, direct, diag_send).wait()

        for y_from in order:
            relay(y_from).wait_recv()


def product_kernel(n_space, polar, coulomb, pattern, sides, screened, out_sides, out_screened, out_sem):
    size = coulomb.shape[-1]
    s = lax.axis_index("space")
    high = s % 2

    def coupling(upper):
        present = jnp.where(jnp.where(upper == 1, s < n_space - 1, s > 0), pattern[0, upper], 0)
        return (coulomb[2 * upper].astype(jnp.float32) * present.astype(jnp.float32)).astype(BF16)

    def image(weight, slot):
        wide = jnp.concatenate([polar[slot, i].reshape(size, size) for i in range(4)], axis=1)
        return jnp.dot(weight, wide, preferred_element_type=jnp.float32).astype(BF16)

    weights = (coulomb[1], coupling(1 - high), coupling(high))
    images = [image(weight, slot) for slot, weight in enumerate(weights)]
    copies = []
    for slot, block in ((1, 1 - high), (2, high)):
        for i in range(4):
            out_sides[slot - 1, i] = images[slot][:, i * size:(i + 1) * size]
        for kind in range(2):
            copies.append(
                pltpu.make_async_copy(
                    out_sides.at[slot - 1, pl.ds(2 * kind, 2)], sides.at[kind, block], out_sem.at[len(copies)]
                )
            )
            copies[-1].start()
    joined_weights = jnp.concatenate(weights, axis=1)
    for i in range(4):
        joined = jnp.concatenate([part[:, i * size:(i + 1) * size] for part in images], axis=1)
        out_screened[i] = lax.dot_general(
            joined, joined_weights, (((1,), (1,)), ((), ())), preferred_element_type=jnp.float32
        ).astype(BF16)
    copies.append(pltpu.make_async_copy(out_screened, screened, out_sem.at[len(copies)]))
    copies[-1].start()
    for copy in copies:
        copy.wait()


def solution(mesh):
    n_energy, n_space = mesh.shape["energy"], mesh.shape["space"]

    def local(greens, coulomb, pattern):
        size = greens.shape[-1]
        rows = size // n_energy
        forward, inverse = make_tables(n_energy, rows)
        anywhere = pl.BlockSpec(memory_space=pl.ANY)
        vmem = pl.BlockSpec(memory_space=pltpu.VMEM)
        dma = pltpu.SemaphoreType.DMA
        strips = n_energy // 4
        polar = pl.pallas_call(
            lambda *refs: exchange_kernel(n_energy, n_space, rows, *refs),
            out_shape=pltpu.VMEM((3, 4, 2, size // 2, size), BF16),
            in_specs=[anywhere] * 3,
            out_specs=vmem,
            scratch_shapes=[
                pltpu.VMEM((4, 2, size, size), BF16),
                pltpu.VMEM((4, 2, size, size), BF16),
                pltpu.VMEM((strips, 4, 2, 4 * rows, size), BF16),
                pltpu.VMEM(forward.shape, BF16),
                pltpu.VMEM(inverse.shape, BF16),
                dma, dma, dma, dma((strips,)), dma, dma, dma, dma((strips,)), dma, dma((strips,)), dma, dma((3,)),
            ],
            compiler_params=pltpu.CompilerParams(collective_id=0, has_side_effects=True),
            name="exchange",
        )(greens.reshape(4, 2, size // 2, size), jnp.asarray(forward), jnp.asarray(inverse))
        sides, screened = pl.pallas_call(
            lambda *refs: product_kernel(n_space, *refs),
            out_shape=(
                jax.ShapeDtypeStruct((2, 2, 2, size, size), BF16),
                jax.ShapeDtypeStruct((4, size, size), BF16),
            ),
            in_specs=[vmem, vmem, pl.BlockSpec(memory_space=pltpu.SMEM)],
            out_specs=(anywhere, anywhere),
            scratch_shapes=[
                pltpu.VMEM((2, 4, size, size), BF16),
                pltpu.VMEM((4, size, size), BF16),
                dma((5,)),
            ],
            compiler_params=pltpu.CompilerParams(vmem_limit_bytes=16 << 20),
            name="products",
        )(polar, coulomb.reshape(3, size, size), pattern)
        return sides.reshape(2, 2, 2, 1, size, size), screened.reshape(2, 2, 1, size, size)

    return jax.shard_map(
        local,
        mesh=mesh,
        in_specs=(P(None, None, "energy", "space", None), P(None, "space", None), P("space", None)),
        out_specs=(P(None, None, None, "energy", "space", None), P(None, None, "energy", "space", None)),
        check_vma=False,
    )
```

```python
import math

import jax
import jax.numpy as jnp
import numpy as np
from jax import lax
from jax.experimental import pallas as pl
from jax.experimental.pallas import tpu as pltpu
from jax.sharding import PartitionSpec as P

MESH = pl.DeviceIdType.MESH
BF16 = jnp.bfloat16
DIRECT = 5


def make_tables(energies, rows):
    period = 2 * energies
    phases = (np.arange(period)[:, None] * np.arange(energies)[None, :] % period) * (2.0 * math.pi / period)
    cos_part, sin_part = np.cos(phases), np.sin(phases)
    forward = np.block([[cos_part, sin_part], [-sin_part, cos_part]])
    cos_back, sin_back = cos_part.T, sin_part.T
    inverse = np.block(
        [[cos_back, -sin_back], [sin_back, cos_back], [-cos_back, -sin_back], [-sin_back, cos_back]]
    ) * (1.0 / (period * math.sqrt(energies)))
    unit = np.eye(rows)
    return tuple(np.kron(table, unit).astype(np.float32).astype(BF16) for table in (forward, inverse))


def exchange_kernel(
    n_energy, n_space, rows,
    greens, forward, inverse,
    polar,
    gathered, spectra, staged, fwd, inv,
    gather_send, gather_sem, stage_send, stage_sem, own_send, own_sem, x_send, x_sem, z_send, z_sem, diag_send, local_sem, x_open, z_open,
):
    e = lax.axis_index("energy")
    s = lax.axis_index("space")
    n_y = n_energy // 4
    core, x, y = e % 2, (e // 2) % 2, e // 4
    high, z = s % 2, s // 2
    n_z = n_space // 2
    mine = e // 2
    partner = s + 1 - 2 * high
    z_to, z_from = s + 2 - 4 * high, s - 2 + 4 * high
    diagonal = s - 1 + 2 * high
    relays = jnp.where(high == 0, z < n_z - 1, z > 0)
    receives = jnp.where(high == 0, z > 0, z < n_z - 1)
    near = []
    for d in range(1, n_y // 2):
        near += [d, -d]
    near.append(n_y // 2)
    far = near[::-1]

    def part(ref, index):
        return ref.at[:, :, pl.ds(pl.multiple_of(index * rows, rows), rows), :]

    def strip(ref, y_from):
        return ref.at[:, :, pl.ds(pl.multiple_of(y_from * 2 * rows, 2 * rows), 2 * rows), :]

    def at_distance(d):
        return (y + d + n_y) % n_y

    def device(y_to, x_to, core_to):
        return 4 * y_to + 2 * x_to + core_to

    barrier = pltpu.get_barrier_semaphore()

    @pl.when(core == 1)
    def _():
        def greet(to):
            pl.semaphore_signal(barrier, inc=1, device_id={"energy": to}, device_id_type=MESH)

        for d in far:
            for x_to in range(2):
                for c in range(2):
                    greet(device(at_distance(d), x_to, c))
        greet(device(y, 1 - x, 0))
        greet(device(y, 1 - x, 1))
        greet(e - 1)
        pl.semaphore_signal(barrier, inc=1, device_id={"space": partner}, device_id_type=MESH)

        @pl.when(receives)
        def _():
            pl.semaphore_signal(barrier, inc=1, device_id={"space": diagonal}, device_id_type=MESH)

    @pl.when(receives)
    def _():
        pl.semaphore_signal(barrier, inc=1, device_id={"space": z_from}, device_id_type=MESH)

    @pl.when(core == 1)
    def _():
        pltpu.make_async_copy(forward, fwd, local_sem.at[0]).start()
        pltpu.make_async_copy(inverse, inv, local_sem.at[1]).start()

    pl.semaphore_wait(
        barrier,
        n_energy // 2 + jnp.where(relays, 1, 0) + jnp.where(receives, core, 0),
    )

    def give(to):
        pltpu.make_async_remote_copy(
            src_ref=part(greens, to),
            dst_ref=part(gathered, e),
            send_sem=gather_send,
            recv_sem=gather_sem,
            device_id={"energy": 2 * to + 1},
            device_id_type=MESH,
        ).start()

    for d in far:
        for across in (1, 0):
            give(2 * at_distance(d) + (x + across) % 2)
    give(2 * y + 1 - x)

    @pl.when(core == 0)
    def _():
        give(mine)

    @pl.when(jnp.logical_not(receives))
    def _():
        polar[2] = jnp.zeros(polar.shape[1:], BF16)

    def stage(y_from, y_to):
        block = 4 * rows
        return pltpu.make_async_remote_copy(
            src_ref=spectra.at[:, :, pl.ds(pl.multiple_of(y_to * block, block), block), :],
            dst_ref=staged.at[y_from],
            send_sem=stage_send,
            recv_sem=stage_sem.at[y_from],
            device_id={"energy": device(y_to, x, 1)},
            device_id_type=MESH,
        )

    def hand_out(y_from, piece, direct):
        index = 2 * y_from + x
        if direct:
            @pl.when(receives)
            def _():
                for x_to in range(2):
                    for c in range(2):
                        pltpu.make_async_remote_copy(
                            src_ref=piece(2 * x_to + c),
                            dst_ref=part(polar.at[2], index),
                            send_sem=diag_send,
                            recv_sem=z_sem.at[y_from],
                            device_id={"energy": device(y, x_to, c), "space": diagonal},
                            device_id_type=MESH,
                        ).start()

        for across in (0, 1):
            for c in (0, 1):
                x_to = (x + across) % 2
                pltpu.make_async_remote_copy(
                    src_ref=piece(2 * x_to + c),
                    dst_ref=part(polar.at[1], index),
                    send_sem=x_send,
                    recv_sem=x_sem.at[y_from],
                    device_id={"energy": device(y, x_to, c), "space": partner},
                    device_id_type=MESH,
                ).start()
        for across, c in ((1, 0), (1, 1), (0, 0)):
            x_to = (x + across) % 2
            pltpu.make_async_remote_copy(
                src_ref=piece(2 * x_to + c),
                dst_ref=part(polar.at[0], index),
                send_sem=own_send,
                recv_sem=own_sem,
                device_id={"energy": device(y, x_to, c)},
                device_id_type=MESH,
            ).start()
        pltpu.make_async_copy(piece(2 * x + 1), part(polar.at[0], index), local_sem.at[2]).start()

    @pl.when(core == 1)
    def _():
        own = pltpu.make_async_copy(part(greens, mine), part(gathered, e), local_sem.at[2])
        own.start()
        pltpu.make_async_copy(forward, fwd, local_sem.at[0]).wait()
        pltpu.make_async_copy(inverse, inv, local_sem.at[1]).wait()
        own.wait()
        others = gathered.at[:, :, pl.ds(0, (n_energy - 1) * rows), :]
        pltpu.make_async_copy(others, others, gather_sem).wait()
        pl.semaphore_signal(x_open, inc=1, device_id={"space": partner}, device_id_type=MESH)

        @pl.when(receives)
        def _():
            pl.semaphore_signal(z_open, inc=1, device_id={"space": diagonal}, device_id_type=MESH)

        size = gathered.shape[-1]
        half = 2 * size
        stacked = jnp.concatenate(
            [
                jnp.concatenate([gathered[2 * a, h], gathered[2 * a + 1, h]], axis=0)
                for a in range(2)
                for h in range(2)
            ],
            axis=1,
        )
        fields = jnp.dot(fwd[...], stacked, preferred_element_type=jnp.float32)
        less_re, less_im = fields[:half, :half], fields[half:, :half]
        great_re, great_im = fields[:half, half:], fields[half:, half:]
        product = jnp.concatenate(
            [less_re * great_im - less_im * great_re, less_re * great_re + less_im * great_im], axis=0
        ).astype(BF16)
        result = jnp.dot(inv[...], product, preferred_element_type=jnp.float32).astype(BF16)
        for i in range(4):
            for h in range(2):
                spectra[i, h] = result[i * size:(i + 1) * size, h * size:(h + 1) * size]

        for d in (1, -1, 2, -2, 4, 3, -3):
            stage(y, at_distance(d)).start()
        pl.semaphore_wait(x_open, 1)

        @pl.when(receives)
        def _():
            pl.semaphore_wait(z_open, 1)

        hand_out(y, lambda j: part(spectra, 4 * y + j), False)
        for i, d in enumerate(near):
            y_from = at_distance(d)
            stage(y_from, y_from).wait_recv()
            hand_out(y_from, lambda j: staged.at[y_from, :, :, pl.ds(j * rows, rows), :], i >= n_y - 1 - DIRECT)

    def relay(y_from):
        return pltpu.make_async_remote_copy(
            src_ref=strip(polar.at[1], y_from),
            dst_ref=strip(polar.at[2], y_from),
            send_sem=z_send,
            recv_sem=z_sem.at[y_from],
            device_id={"space": z_to},
            device_id_type=MESH,
        )

    order = [y] + [at_distance(d) for d in near]
    for i, y_from in enumerate(order):
        landed = strip(polar.at[1], y_from)
        pltpu.make_async_copy(landed, landed, x_sem.at[y_from]).wait()
        if i < n_y - DIRECT:
            @pl.when(relays)
            def _():
                relay(y_from).start()

    half_own = polar.at[0, pl.ds(0, 2)]

    @pl.when(core == 0)
    def _():
        pltpu.make_async_copy(polar.at[0], polar.at[0], own_sem).wait()

    @pl.when(core == 1)
    def _():
        pltpu.make_async_copy(half_own, half_own, own_sem).wait()
        pltpu.make_async_copy(half_own, half_own, local_sem.at[2]).wait()

    sent = gathered.at[:, :, pl.ds(0, (n_energy // 2 - 1) * rows), :]
    pltpu.make_async_copy(sent, sent, gather_send).wait()

    @pl.when(core == 0)
    def _():
        one = part(polar.at[0], 0)
        pltpu.make_async_copy(one, one, gather_send).wait()

    @pl.when(core == 1)
    def _():
        back = spectra.at[:, :, pl.ds(0, (n_y - 1) * 4 * rows), :]
        pltpu.make_async_copy(back, back, stage_send).wait()
        six = staged.at[pl.ds(0, 6)]
        pltpu.make_async_copy(six, six, own_send).wait()
        two = polar.at[pl.ds(0, 2)]
        pltpu.make_async_copy(two, two, x_send).wait()

    @pl.when(relays)
    def _():
        relayed = polar.at[1, :, :, pl.ds(0, (n_y - DIRECT) * 2 * rows), :]
        pltpu.make_async_copy(relayed, relayed, z_send).wait()

    @pl.when(receives)
    def _():
        if DIRECT > 0:
            @pl.when(core == 1)
            def _():
                direct = staged.at[pl.ds(0, DIRECT)]
                pltpu.make_async_copy(direct, direct, diag_send).wait()

        for y_from in order:
            relay(y_from).wait_recv()


def product_kernel(n_space, polar, coulomb, pattern, sides, screened, out_sides, out_screened, out_sem):
    size = coulomb.shape[-1]
    s = lax.axis_index("space")
    high = s % 2

    def coupling(upper):
        present = jnp.where(jnp.where(upper == 1, s < n_space - 1, s > 0), pattern[0, upper], 0)
        return (coulomb[2 * upper].astype(jnp.float32) * present.astype(jnp.float32)).astype(BF16)

    def image(weight, slot):
        wide = jnp.concatenate([polar[slot, i].reshape(size, size) for i in range(4)], axis=1)
        return jnp.dot(weight, wide, preferred_element_type=jnp.float32).astype(BF16)

    weights = (coulomb[1], coupling(1 - high), coupling(high))
    images = [image(weight, slot) for slot, weight in enumerate(weights)]
    copies = []
    for slot, block in ((1, 1 - high), (2, high)):
        for i in range(4):
            out_sides[slot - 1, i] = images[slot][:, i * size:(i + 1) * size]
        for kind in range(2):
            copies.append(
                pltpu.make_async_copy(
                    out_sides.at[slot - 1, pl.ds(2 * kind, 2)], sides.at[kind, block], out_sem.at[len(copies)]
                )
            )
            copies[-1].start()
    joined_weights = jnp.concatenate(weights, axis=1)
    for i in range(4):
        joined = jnp.concatenate([part[:, i * size:(i + 1) * size] for part in images], axis=1)
        out_screened[i] = lax.dot_general(
            joined, joined_weights, (((1,), (1,)), ((), ())), preferred_element_type=jnp.float32
        ).astype(BF16)
    copies.append(pltpu.make_async_copy(out_screened, screened, out_sem.at[len(copies)]))
    copies[-1].start()
    for copy in copies:
        copy.wait()


def solution(mesh):
    n_energy, n_space = mesh.shape["energy"], mesh.shape["space"]

    def local(greens, coulomb, pattern):
        size = greens.shape[-1]
        rows = size // n_energy
        forward, inverse = make_tables(n_energy, rows)
        anywhere = pl.BlockSpec(memory_space=pl.ANY)
        vmem = pl.BlockSpec(memory_space=pltpu.VMEM)
        dma = pltpu.SemaphoreType.DMA
        strips = n_energy // 4
        polar = pl.pallas_call(
            lambda *refs: exchange_kernel(n_energy, n_space, rows, *refs),
            out_shape=pltpu.VMEM((3, 4, 2, size // 2, size), BF16),
            in_specs=[anywhere] * 3,
            out_specs=vmem,
            scratch_shapes=[
                pltpu.VMEM((4, 2, size, size), BF16),
                pltpu.VMEM((4, 2, size, size), BF16),
                pltpu.VMEM((strips, 4, 2, 4 * rows, size), BF16),
                pltpu.VMEM(forward.shape, BF16),
                pltpu.VMEM(inverse.shape, BF16),
                dma, dma, dma, dma((strips,)), dma, dma, dma, dma((strips,)), dma, dma((strips,)), dma, dma((3,)),
                pltpu.SemaphoreType.REGULAR, pltpu.SemaphoreType.REGULAR,
            ],
            compiler_params=pltpu.CompilerParams(collective_id=0, has_side_effects=True),
            name="exchange",
        )(greens.reshape(4, 2, size // 2, size), jnp.asarray(forward), jnp.asarray(inverse))
        sides, screened = pl.pallas_call(
            lambda *refs: product_kernel(n_space, *refs),
            out_shape=(
                jax.ShapeDtypeStruct((2, 2, 2, size, size), BF16),
                jax.ShapeDtypeStruct((4, size, size), BF16),
            ),
            in_specs=[vmem, vmem, pl.BlockSpec(memory_space=pltpu.SMEM)],
            out_specs=(anywhere, anywhere),
            scratch_shapes=[
                pltpu.VMEM((2, 4, size, size), BF16),
                pltpu.VMEM((4, size, size), BF16),
                dma((5,)),
            ],
            compiler_params=pltpu.CompilerParams(vmem_limit_bytes=16 << 20),
            name="products",
        )(polar, coulomb.reshape(3, size, size), pattern)
        return sides.reshape(2, 2, 2, 1, size, size), screened.reshape(2, 2, 1, size, size)

    return jax.shard_map(
        local,
        mesh=mesh,
        in_specs=(P(None, None, "energy", "space", None), P(None, "space", None), P("space", None)),
        out_specs=(P(None, None, None, "energy", "space", None), P(None, None, "energy", "space", None)),
        check_vma=False,
    )
```

```python
import math

import jax
import jax.numpy as jnp
import numpy as np
from jax import lax
from jax.experimental import pallas as pl
from jax.experimental.pallas import tpu as pltpu
from jax.sharding import PartitionSpec as P

MESH = pl.DeviceIdType.MESH
BF16 = jnp.bfloat16
KEEP = 8


def make_tables(energies, rows):
    period = 2 * energies
    phases = (np.arange(period)[:, None] * np.arange(energies)[None, :] % period) * (2.0 * math.pi / period)
    cos_part, sin_part = np.cos(phases), np.sin(phases)
    forward = np.block([[cos_part, sin_part], [-sin_part, cos_part]])
    cos_back, sin_back = cos_part.T, sin_part.T
    inverse = np.block(
        [[cos_back, -sin_back], [sin_back, cos_back], [-cos_back, -sin_back], [-sin_back, cos_back]]
    ) * (1.0 / (period * math.sqrt(energies)))
    unit = np.eye(rows)
    return tuple(np.kron(table, unit).astype(np.float32).astype(BF16) for table in (forward, inverse))


def exchange_kernel(
    n_energy, n_space, rows,
    greens, forward, inverse,
    polar,
    gathered, spectra, staged, fwd, inv,
    gather_send, gather_sem, stage_send, stage_sem, own_send, own_sem, x_send, x_sem, z_send, z_sem, local_sem, x_open, z_open,
):
    e = lax.axis_index("energy")
    s = lax.axis_index("space")
    n_y = n_energy // 4
    core, x, y = e % 2, (e // 2) % 2, e // 4
    high, z = s % 2, s // 2
    n_z = n_space // 2
    mine = e // 2
    partner = s + 1 - 2 * high
    diagonal = s - 1 + 2 * high
    reaches = jnp.where(high == 0, z > 0, z < n_z - 1)
    near = []
    for d in range(1, n_y // 2):
        near += [d, -d]
    near.append(n_y // 2)
    far = near[::-1]

    def part(ref, index):
        return ref.at[:, :, pl.ds(pl.multiple_of(index * rows, rows), rows), :]

    def at_distance(d):
        return (y + d + n_y) % n_y

    def device(y_to, x_to, core_to):
        return 4 * y_to + 2 * x_to + core_to

    barrier = pltpu.get_barrier_semaphore()

    @pl.when(core == 1)
    def _():
        def greet(to):
            pl.semaphore_signal(barrier, inc=1, device_id={"energy": to}, device_id_type=MESH)

        for d in far:
            for x_to in range(2):
                for c in range(2):
                    greet(device(at_distance(d), x_to, c))
        greet(device(y, 1 - x, 0))
        greet(device(y, 1 - x, 1))
        greet(e - 1)
        pl.semaphore_signal(barrier, inc=1, device_id={"space": partner}, device_id_type=MESH)

        @pl.when(reaches)
        def _():
            pl.semaphore_signal(barrier, inc=1, device_id={"space": diagonal}, device_id_type=MESH)

    @pl.when(core == 1)
    def _():
        pltpu.make_async_copy(forward, fwd, local_sem.at[0]).start()
        pltpu.make_async_copy(inverse, inv, local_sem.at[1]).start()

    pl.semaphore_wait(
        barrier,
        n_energy // 2 + jnp.where(reaches, core, 0),
    )

    def give(to):
        pltpu.make_async_remote_copy(
            src_ref=part(greens, to),
            dst_ref=part(gathered, e),
            send_sem=gather_send,
            recv_sem=gather_sem,
            device_id={"energy": 2 * to + 1},
            device_id_type=MESH,
        ).start()

    for d in far:
        for across in (1, 0):
            give(2 * at_distance(d) + (x + across) % 2)
    give(2 * y + 1 - x)

    @pl.when(core == 0)
    def _():
        give(mine)

    @pl.when(jnp.logical_not(reaches))
    def _():
        polar[2] = jnp.zeros(polar.shape[1:], BF16)

    def stage(y_from, y_to):
        block = 4 * rows
        return pltpu.make_async_remote_copy(
            src_ref=spectra.at[:, :, pl.ds(pl.multiple_of(y_to * block, block), block), :],
            dst_ref=staged.at[y_from],
            send_sem=stage_send,
            recv_sem=stage_sem.at[y_from],
            device_id={"energy": device(y_to, x, 1)},
            device_id_type=MESH,
        )

    def pass_on(y_from, piece):
        index = 2 * y_from + x

        def give_to(slot, row, send, recv):
            for across in (0, 1):
                for c in (0, 1):
                    x_to = (x + across) % 2
                    pltpu.make_async_remote_copy(
                        src_ref=piece(2 * x_to + c),
                        dst_ref=part(polar.at[slot], index),
                        send_sem=send,
                        recv_sem=recv,
                        device_id={"energy": device(y, x_to, c), "space": row},
                        device_id_type=MESH,
                    ).start()

        @pl.when(reaches)
        def _():
            give_to(2, diagonal, z_send, z_sem)

        give_to(1, partner, x_send, x_sem)

    def hand_out(y_from, piece):
        index = 2 * y_from + x
        for across, c in ((1, 0), (1, 1), (0, 0)):
            x_to = (x + across) % 2
            pltpu.make_async_remote_copy(
                src_ref=piece(2 * x_to + c),
                dst_ref=part(polar.at[0], index),
                send_sem=own_send,
                recv_sem=own_sem,
                device_id={"energy": device(y, x_to, c)},
                device_id_type=MESH,
            ).start()
        pltpu.make_async_copy(piece(2 * x + 1), part(polar.at[0], index), local_sem.at[2]).start()

    @pl.when(core == 1)
    def _():
        own = pltpu.make_async_copy(part(greens, mine), part(gathered, e), local_sem.at[2])
        own.start()
        pltpu.make_async_copy(forward, fwd, local_sem.at[0]).wait()
        pltpu.make_async_copy(inverse, inv, local_sem.at[1]).wait()
        own.wait()
        others = gathered.at[:, :, pl.ds(0, (n_energy - 1) * rows), :]
        pltpu.make_async_copy(others, others, gather_sem).wait()
        pl.semaphore_signal(x_open, inc=1, device_id={"space": partner}, device_id_type=MESH)

        @pl.when(reaches)
        def _():
            pl.semaphore_signal(z_open, inc=1, device_id={"space": diagonal}, device_id_type=MESH)

        size = gathered.shape[-1]
        half = 2 * size
        stacked = jnp.concatenate(
            [
                jnp.concatenate([gathered[2 * a, h], gathered[2 * a + 1, h]], axis=0)
                for a in range(2)
                for h in range(2)
            ],
            axis=1,
        )
        fields = jnp.dot(fwd[...], stacked, preferred_element_type=jnp.float32)
        less_re, less_im = fields[:half, :half], fields[half:, :half]
        great_re, great_im = fields[:half, half:], fields[half:, half:]
        product = jnp.concatenate(
            [less_re * great_im - less_im * great_re, less_re * great_re + less_im * great_im], axis=0
        ).astype(BF16)
        result = jnp.dot(inv[...], product, preferred_element_type=jnp.float32).astype(BF16)
        for i in range(4):
            for h in range(2):
                spectra[i, h] = result[i * size:(i + 1) * size, h * size:(h + 1) * size]

        for d in (1, -1, 2, -2, 4, 3, -3):
            stage(y, at_distance(d)).start()
        pl.semaphore_wait(x_open, 1)

        @pl.when(reaches)
        def _():
            pl.semaphore_wait(z_open, 1)

        pieces = [(y, lambda j: part(spectra, 4 * y + j))]
        for d in near:
            y_from = at_distance(d)
            pieces.append((y_from, lambda j, y_from=y_from: staged.at[y_from, :, :, pl.ds(j * rows, rows), :]))
        for i, (y_from, piece) in enumerate(pieces):
            if i > 0:
                stage(y_from, y_from).wait_recv()
            pass_on(y_from, piece)
            if i < KEEP:
                hand_out(y_from, piece)
        for y_from, piece in pieces[KEEP:]:
            hand_out(y_from, piece)

    half_own = polar.at[0, pl.ds(0, 2)]

    @pl.when(core == 0)
    def _():
        pltpu.make_async_copy(polar.at[0], polar.at[0], own_sem).wait()

    @pl.when(core == 1)
    def _():
        pltpu.make_async_copy(half_own, half_own, own_sem).wait()
        pltpu.make_async_copy(half_own, half_own, local_sem.at[2]).wait()

    sent = gathered.at[:, :, pl.ds(0, (n_energy // 2 - 1) * rows), :]
    pltpu.make_async_copy(sent, sent, gather_send).wait()

    @pl.when(core == 0)
    def _():
        one = part(polar.at[0], 0)
        pltpu.make_async_copy(one, one, gather_send).wait()

    @pl.when(core == 1)
    def _():
        back = spectra.at[:, :, pl.ds(0, (n_y - 1) * 4 * rows), :]
        pltpu.make_async_copy(back, back, stage_send).wait()
        six = staged.at[pl.ds(0, 6)]
        pltpu.make_async_copy(six, six, own_send).wait()
        pltpu.make_async_copy(staged, staged, x_send).wait()

        @pl.when(reaches)
        def _():
            pltpu.make_async_copy(staged, staged, z_send).wait()

    pltpu.make_async_copy(polar.at[1], polar.at[1], x_sem).wait()

    @pl.when(reaches)
    def _():
        pltpu.make_async_copy(polar.at[2], polar.at[2], z_sem).wait()


def product_kernel(n_space, polar, coulomb, pattern, sides, screened, out_sides, out_screened, out_sem):
    size = coulomb.shape[-1]
    s = lax.axis_index("space")
    high = s % 2

    present = pattern[...].astype(jnp.float32)
    below = present[:, 0:1] * jnp.where(s > 0, 1.0, 0.0)
    above = present[:, 1:2] * jnp.where(s < n_space - 1, 1.0, 0.0)

    def coupling(upper):
        mark = jnp.where(upper == 1, above, below)
        return (coulomb[2 * upper].astype(jnp.float32) * mark).astype(BF16)

    def image(weight, slot):
        wide = jnp.concatenate([polar[slot, i].reshape(size, size) for i in range(4)], axis=1)
        return jnp.dot(weight, wide, preferred_element_type=jnp.float32).astype(BF16)

    weights = (coulomb[1], coupling(1 - high), coupling(high))
    copies = []
    images = [image(weights[0], 0)]
    for slot, block in ((1, 1 - high), (2, high)):
        images.append(image(weights[slot], slot))
        for i in range(4):
            out_sides[slot - 1, i // 2, i % 2] = images[slot][:, i * size:(i + 1) * size]
        copies.append(pltpu.make_async_copy(out_sides.at[slot - 1], sides.at[:, block], out_sem.at[slot - 1]))
    joined = jnp.concatenate(
        [jnp.concatenate([part[:, i * size:(i + 1) * size] for part in images], axis=1) for i in range(4)], axis=0
    )
    result = lax.dot_general(
        joined,
        jnp.concatenate(weights, axis=1),
        (((1,), (1,)), ((), ())),
        preferred_element_type=jnp.float32,
    ).astype(BF16)
    for i in range(4):
        out_screened[i] = result[i * size:(i + 1) * size]
    last = pltpu.make_async_copy(out_screened, screened, out_sem.at[2])
    for copy in copies:
        copy.start()
    last.start()
    for copy in copies:
        copy.wait()
    last.wait()


def solution(mesh):
    n_energy, n_space = mesh.shape["energy"], mesh.shape["space"]

    def local(greens, coulomb, pattern):
        size = greens.shape[-1]
        rows = size // n_energy
        forward, inverse = make_tables(n_energy, rows)
        anywhere = pl.BlockSpec(memory_space=pl.ANY)
        vmem = pl.BlockSpec(memory_space=pltpu.VMEM)
        dma = pltpu.SemaphoreType.DMA
        strips = n_energy // 4
        polar = pl.pallas_call(
            lambda *refs: exchange_kernel(n_energy, n_space, rows, *refs),
            out_shape=pltpu.VMEM((3, 4, 2, size // 2, size), BF16),
            in_specs=[anywhere] * 3,
            out_specs=vmem,
            scratch_shapes=[
                pltpu.VMEM((4, 2, size, size), BF16),
                pltpu.VMEM((4, 2, size, size), BF16),
                pltpu.VMEM((strips, 4, 2, 4 * rows, size), BF16),
                pltpu.VMEM(forward.shape, BF16),
                pltpu.VMEM(inverse.shape, BF16),
                dma, dma, dma, dma((strips,)), dma, dma, dma, dma, dma, dma, dma((3,)),
                pltpu.SemaphoreType.REGULAR, pltpu.SemaphoreType.REGULAR,
            ],
            compiler_params=pltpu.CompilerParams(collective_id=0, has_side_effects=True),
            name="exchange",
        )(greens.reshape(4, 2, size // 2, size), jnp.asarray(forward), jnp.asarray(inverse))
        sides, screened = pl.pallas_call(
            lambda *refs: product_kernel(n_space, *refs),
            out_shape=(
                jax.ShapeDtypeStruct((2, 2, 2, size, size), BF16),
                jax.ShapeDtypeStruct((4, size, size), BF16),
            ),
            in_specs=[vmem, vmem, vmem],
            out_specs=(anywhere, anywhere),
            scratch_shapes=[
                pltpu.VMEM((2, 2, 2, size, size), BF16),
                pltpu.VMEM((4, size, size), BF16),
                dma((3,)),
            ],
            compiler_params=pltpu.CompilerParams(vmem_limit_bytes=16 << 20),
            name="products",
        )(polar, coulomb.reshape(3, size, size), pattern)
        return sides.reshape(2, 2, 2, 1, size, size), screened.reshape(2, 2, 1, size, size)

    return jax.shard_map(
        local,
        mesh=mesh,
        in_specs=(P(None, None, "energy", "space", None), P(None, "space", None), P("space", None)),
        out_specs=(P(None, None, None, "energy", "space", None), P(None, None, "energy", "space", None)),
        check_vma=False,
    )
```

```python
import math

import jax
import jax.numpy as jnp
import numpy as np
from jax import lax
from jax.experimental import pallas as pl
from jax.experimental.pallas import tpu as pltpu
from jax.sharding import PartitionSpec as P

MESH = pl.DeviceIdType.MESH
BF16 = jnp.bfloat16
KEEP = 8


def make_tables(energies, rows):
    period = 2 * energies
    phases = (np.arange(period)[:, None] * np.arange(energies)[None, :] % period) * (2.0 * math.pi / period)
    cos_part, sin_part = np.cos(phases), np.sin(phases)
    forward = np.block([[cos_part, sin_part], [-sin_part, cos_part]])
    cos_back, sin_back = cos_part.T, sin_part.T
    inverse = np.block(
        [[cos_back, -sin_back], [sin_back, cos_back], [-cos_back, -sin_back], [-sin_back, cos_back]]
    ) * (1.0 / (period * math.sqrt(energies)))
    unit = np.eye(rows)
    return tuple(np.kron(table, unit).astype(np.float32).astype(BF16) for table in (forward, inverse))


def exchange_kernel(
    n_energy, n_space, rows,
    greens, forward, inverse,
    polar,
    gathered, spectra, staged, fwd, inv, held,
    gather_send, gather_sem, stage_send, stage_sem, own_send, own_sem, x_send, x_sem, z_send, z_sem, local_sem, x_open, z_open,
):
    e = lax.axis_index("energy")
    s = lax.axis_index("space")
    n_y = n_energy // 4
    core, x, y = e % 2, (e // 2) % 2, e // 4
    high, z = s % 2, s // 2
    n_z = n_space // 2
    mine = e // 2
    partner = s + 1 - 2 * high
    diagonal = s - 1 + 2 * high
    reaches = jnp.where(high == 0, z > 0, z < n_z - 1)
    near = []
    for d in range(1, n_y // 2):
        near += [d, -d]
    near.append(n_y // 2)
    far = near[::-1]

    def part(ref, index):
        return ref.at[:, :, pl.ds(pl.multiple_of(index * rows, rows), rows), :]

    def at_distance(d):
        return (y + d + n_y) % n_y

    def device(y_to, x_to, core_to):
        return 4 * y_to + 2 * x_to + core_to

    hold = pltpu.make_async_copy(greens, held, local_sem.at[3])
    hold.start()
    barrier = pltpu.get_barrier_semaphore()

    @pl.when(core == 1)
    def _():
        def greet(to):
            pl.semaphore_signal(barrier, inc=1, device_id={"energy": to}, device_id_type=MESH)

        for d in far:
            for x_to in range(2):
                for c in range(2):
                    greet(device(at_distance(d), x_to, c))
        greet(device(y, 1 - x, 0))
        greet(device(y, 1 - x, 1))
        greet(e - 1)
        pl.semaphore_signal(barrier, inc=1, device_id={"space": partner}, device_id_type=MESH)

        @pl.when(reaches)
        def _():
            pl.semaphore_signal(barrier, inc=1, device_id={"space": diagonal}, device_id_type=MESH)

    @pl.when(core == 1)
    def _():
        pltpu.make_async_copy(forward, fwd, local_sem.at[0]).start()
        pltpu.make_async_copy(inverse, inv, local_sem.at[1]).start()

    pl.semaphore_wait(
        barrier,
        n_energy // 2 + jnp.where(reaches, core, 0),
    )

    hold.wait()

    def give(to):
        pltpu.make_async_remote_copy(
            src_ref=part(held, to),
            dst_ref=part(gathered, e),
            send_sem=gather_send,
            recv_sem=gather_sem,
            device_id={"energy": 2 * to + 1},
            device_id_type=MESH,
        ).start()

    for d in far:
        for across in (1, 0):
            give(2 * at_distance(d) + (x + across) % 2)
    give(2 * y + 1 - x)

    @pl.when(core == 0)
    def _():
        give(mine)

    @pl.when(jnp.logical_not(reaches))
    def _():
        polar[2] = jnp.zeros(polar.shape[1:], BF16)

    def stage(y_from, y_to):
        block = 4 * rows
        return pltpu.make_async_remote_copy(
            src_ref=spectra.at[:, :, pl.ds(pl.multiple_of(y_to * block, block), block), :],
            dst_ref=staged.at[y_from],
            send_sem=stage_send,
            recv_sem=stage_sem.at[y_from],
            device_id={"energy": device(y_to, x, 1)},
            device_id_type=MESH,
        )

    def pass_on(y_from, piece):
        index = 2 * y_from + x

        def give_to(slot, row, send, recv):
            for across in (0, 1):
                for c in (0, 1):
                    x_to = (x + across) % 2
                    pltpu.make_async_remote_copy(
                        src_ref=piece(2 * x_to + c),
                        dst_ref=part(polar.at[slot], index),
                        send_sem=send,
                        recv_sem=recv,
                        device_id={"energy": device(y, x_to, c), "space": row},
                        device_id_type=MESH,
                    ).start()

        @pl.when(reaches)
        def _():
            give_to(2, diagonal, z_send, z_sem)

        give_to(1, partner, x_send, x_sem)

    def hand_out(y_from, piece):
        index = 2 * y_from + x
        for across, c in ((1, 0), (1, 1), (0, 0)):
            x_to = (x + across) % 2
            pltpu.make_async_remote_copy(
                src_ref=piece(2 * x_to + c),
                dst_ref=part(polar.at[0], index),
                send_sem=own_send,
                recv_sem=own_sem,
                device_id={"energy": device(y, x_to, c)},
                device_id_type=MESH,
            ).start()
        pltpu.make_async_copy(piece(2 * x + 1), part(polar.at[0], index), local_sem.at[2]).start()

    @pl.when(core == 1)
    def _():
        own = pltpu.make_async_copy(part(held, mine), part(gathered, e), local_sem.at[2])
        own.start()
        pltpu.make_async_copy(forward, fwd, local_sem.at[0]).wait()
        pltpu.make_async_copy(inverse, inv, local_sem.at[1]).wait()
        own.wait()
        others = gathered.at[:, :, pl.ds(0, (n_energy - 1) * rows), :]
        pltpu.make_async_copy(others, others, gather_sem).wait()
        pl.semaphore_signal(x_open, inc=1, device_id={"space": partner}, device_id_type=MESH)

        @pl.when(reaches)
        def _():
            pl.semaphore_signal(z_open, inc=1, device_id={"space": diagonal}, device_id_type=MESH)

        size = gathered.shape[-1]
        half = 2 * size
        stacked = jnp.concatenate(
            [
                jnp.concatenate([gathered[2 * a, h], gathered[2 * a + 1, h]], axis=0)
                for a in range(2)
                for h in range(2)
            ],
            axis=1,
        )
        real_parts, imag_parts = [], []
        step = half // 2
        for c in range(2):
            real = jnp.dot(fwd[c * step:(c + 1) * step], stacked, preferred_element_type=jnp.float32)
            imag = jnp.dot(fwd[half + c * step:half + (c + 1) * step], stacked, preferred_element_type=jnp.float32)
            less_re, less_im = real[:, :half], imag[:, :half]
            great_re, great_im = real[:, half:], imag[:, half:]
            real_parts.append((less_re * great_im - less_im * great_re).astype(BF16))
            imag_parts.append((less_re * great_re + less_im * great_im).astype(BF16))
        product = jnp.concatenate(real_parts + imag_parts, axis=0)
        result = jnp.dot(inv[...], product, preferred_element_type=jnp.float32).astype(BF16)
        for i in range(4):
            for h in range(2):
                spectra[i, h] = result[i * size:(i + 1) * size, h * size:(h + 1) * size]

        for d in (1, -1, 2, -2, 4, 3, -3):
            stage(y, at_distance(d)).start()
        pl.semaphore_wait(x_open, 1)

        @pl.when(reaches)
        def _():
            pl.semaphore_wait(z_open, 1)

        pieces = [(y, lambda j: part(spectra, 4 * y + j))]
        for d in near:
            y_from = at_distance(d)
            pieces.append((y_from, lambda j, y_from=y_from: staged.at[y_from, :, :, pl.ds(j * rows, rows), :]))
        for i, (y_from, piece) in enumerate(pieces):
            if i > 0:
                stage(y_from, y_from).wait_recv()
            pass_on(y_from, piece)
            if i < KEEP:
                hand_out(y_from, piece)
        for y_from, piece in pieces[KEEP:]:
            hand_out(y_from, piece)

    half_own = polar.at[0, pl.ds(0, 2)]

    @pl.when(core == 0)
    def _():
        pltpu.make_async_copy(polar.at[0], polar.at[0], own_sem).wait()

    @pl.when(core == 1)
    def _():
        pltpu.make_async_copy(half_own, half_own, own_sem).wait()
        pltpu.make_async_copy(half_own, half_own, local_sem.at[2]).wait()

    sent = gathered.at[:, :, pl.ds(0, (n_energy // 2 - 1) * rows), :]
    pltpu.make_async_copy(sent, sent, gather_send).wait()

    @pl.when(core == 0)
    def _():
        one = part(polar.at[0], 0)
        pltpu.make_async_copy(one, one, gather_send).wait()

    @pl.when(core == 1)
    def _():
        back = spectra.at[:, :, pl.ds(0, (n_y - 1) * 4 * rows), :]
        pltpu.make_async_copy(back, back, stage_send).wait()
        six = staged.at[pl.ds(0, 6)]
        pltpu.make_async_copy(six, six, own_send).wait()
        pltpu.make_async_copy(staged, staged, x_send).wait()

        @pl.when(reaches)
        def _():
            pltpu.make_async_copy(staged, staged, z_send).wait()

    pltpu.make_async_copy(polar.at[1], polar.at[1], x_sem).wait()

    @pl.when(reaches)
    def _():
        pltpu.make_async_copy(polar.at[2], polar.at[2], z_sem).wait()


def product_kernel(n_space, polar, coulomb, pattern, sides, screened, out_sides, out_screened, out_sem):
    size = coulomb.shape[-1]
    s = lax.axis_index("space")
    high = s % 2

    present = pattern[...].astype(jnp.float32)
    below = present[:, 0:1] * jnp.where(s > 0, 1.0, 0.0)
    above = present[:, 1:2] * jnp.where(s < n_space - 1, 1.0, 0.0)

    def coupling(upper):
        mark = jnp.where(upper == 1, above, below)
        return (coulomb[2 * upper].astype(jnp.float32) * mark).astype(BF16)

    def image(weight, slot):
        wide = jnp.concatenate([polar[slot, i].reshape(size, size) for i in range(4)], axis=1)
        return jnp.dot(weight, wide, preferred_element_type=jnp.float32).astype(BF16)

    weights = (coulomb[1], coupling(1 - high), coupling(high))
    copies = []
    images = [image(weights[0], 0)]
    for slot, block in ((1, 1 - high), (2, high)):
        images.append(image(weights[slot], slot))
        for i in range(4):
            out_sides[slot - 1, i // 2, i % 2] = images[slot][:, i * size:(i + 1) * size]
        copies.append(pltpu.make_async_copy(out_sides.at[slot - 1], sides.at[:, block], out_sem.at[slot - 1]))
    joined = jnp.concatenate(
        [jnp.concatenate([part[:, i * size:(i + 1) * size] for part in images], axis=1) for i in range(4)], axis=0
    )
    result = lax.dot_general(
        joined,
        jnp.concatenate(weights, axis=1),
        (((1,), (1,)), ((), ())),
        preferred_element_type=jnp.float32,
    ).astype(BF16)
    for i in range(4):
        out_screened[i] = result[i * size:(i + 1) * size]
    last = pltpu.make_async_copy(out_screened, screened, out_sem.at[2])
    for copy in copies:
        copy.start()
    last.start()
    for copy in copies:
        copy.wait()
    last.wait()


def solution(mesh):
    n_energy, n_space = mesh.shape["energy"], mesh.shape["space"]

    def local(greens, coulomb, pattern):
        size = greens.shape[-1]
        rows = size // n_energy
        forward, inverse = make_tables(n_energy, rows)
        anywhere = pl.BlockSpec(memory_space=pl.ANY)
        vmem = pl.BlockSpec(memory_space=pltpu.VMEM)
        dma = pltpu.SemaphoreType.DMA
        strips = n_energy // 4
        polar = pl.pallas_call(
            lambda *refs: exchange_kernel(n_energy, n_space, rows, *refs),
            out_shape=pltpu.VMEM((3, 4, 2, size // 2, size), BF16),
            in_specs=[anywhere] * 3,
            out_specs=vmem,
            scratch_shapes=[
                pltpu.VMEM((4, 2, size, size), BF16),
                pltpu.VMEM((4, 2, size, size), BF16),
                pltpu.VMEM((strips, 4, 2, 4 * rows, size), BF16),
                pltpu.VMEM(forward.shape, BF16),
                pltpu.VMEM(inverse.shape, BF16),
                pltpu.VMEM((4, 2, size // 2, size), BF16),
                dma, dma, dma, dma((strips,)), dma, dma, dma, dma, dma, dma, dma((4,)),
                pltpu.SemaphoreType.REGULAR, pltpu.SemaphoreType.REGULAR,
            ],
            compiler_params=pltpu.CompilerParams(collective_id=0, has_side_effects=True),
            name="exchange",
        )(greens.reshape(4, 2, size // 2, size), jnp.asarray(forward), jnp.asarray(inverse))
        sides, screened = pl.pallas_call(
            lambda *refs: product_kernel(n_space, *refs),
            out_shape=(
                jax.ShapeDtypeStruct((2, 2, 2, size, size), BF16),
                jax.ShapeDtypeStruct((4, size, size), BF16),
            ),
            in_specs=[vmem, vmem, vmem],
            out_specs=(anywhere, anywhere),
            scratch_shapes=[
                pltpu.VMEM((2, 2, 2, size, size), BF16),
                pltpu.VMEM((4, size, size), BF16),
                dma((3,)),
            ],
            compiler_params=pltpu.CompilerParams(vmem_limit_bytes=16 << 20),
            name="products",
        )(polar, coulomb.reshape(3, size, size), pattern)
        return sides.reshape(2, 2, 2, 1, size, size), screened.reshape(2, 2, 1, size, size)

    return jax.shard_map(
        local,
        mesh=mesh,
        in_specs=(P(None, None, "energy", "space", None), P(None, "space", None), P("space", None)),
        out_specs=(P(None, None, None, "energy", "space", None), P(None, None, "energy", "space", None)),
        check_vma=False,
    )
```

```python
import math

import jax
import jax.numpy as jnp
import numpy as np
from jax import lax
from jax.experimental import pallas as pl
from jax.experimental.pallas import tpu as pltpu
from jax.sharding import PartitionSpec as P

MESH = pl.DeviceIdType.MESH
BF16 = jnp.bfloat16
KEEP = 8


def make_tables(energies, rows):
    period = 2 * energies
    phases = (np.arange(period)[:, None] * np.arange(energies)[None, :] % period) * (2.0 * math.pi / period)
    cos_part, sin_part = np.cos(phases), np.sin(phases)
    forward = np.block([[cos_part, sin_part], [-sin_part, cos_part]])
    cos_back, sin_back = cos_part.T, sin_part.T
    inverse = np.block(
        [[cos_back, -sin_back], [sin_back, cos_back], [-cos_back, -sin_back], [-sin_back, cos_back]]
    ) * (1.0 / (period * math.sqrt(energies)))
    unit = np.eye(rows)
    return tuple(np.kron(table, unit).astype(np.float32).astype(BF16) for table in (forward, inverse))


def exchange_kernel(
    n_energy, n_space, rows,
    greens, forward, inverse,
    polar,
    gathered, spectra, staged, fwd, inv, held,
    gather_send, gather_sem, stage_send, stage_sem, own_send, own_sem, x_send, x_sem, z_send, z_sem, local_sem, x_open, z_open,
):
    e = lax.axis_index("energy")
    s = lax.axis_index("space")
    n_y = n_energy // 4
    core, mine, y = lax.rem(e, 2), lax.div(e, 2), lax.div(e, 4)
    x = mine - 2 * y
    z = lax.div(s, 2)
    high = s - 2 * z
    n_z = n_space // 2
    partner = s + 1 - 2 * high
    diagonal = s - 1 + 2 * high
    reaches = jnp.where(high == 0, z > 0, z < n_z - 1)
    near = []
    for d in range(1, n_y // 2):
        near += [d, -d]
    near.append(n_y // 2)
    far = near[::-1]

    def part(ref, index):
        return ref.at[:, :, pl.ds(pl.multiple_of(index * rows, rows), rows), :]

    def at_distance(d):
        return lax.rem(y + (d + n_y) % n_y, n_y)

    def device(y_to, x_to, core_to):
        return 4 * y_to + 2 * x_to + core_to

    hold = pltpu.make_async_copy(greens, held, local_sem.at[3])
    hold.start()
    barrier = pltpu.get_barrier_semaphore()

    @pl.when(core == 1)
    def _():
        def greet(to):
            pl.semaphore_signal(barrier, inc=1, device_id={"energy": to}, device_id_type=MESH)

        for d in far:
            for x_to in range(2):
                for c in range(2):
                    greet(device(at_distance(d), x_to, c))
        greet(device(y, 1 - x, 0))
        greet(device(y, 1 - x, 1))
        greet(e - 1)
        pl.semaphore_signal(barrier, inc=1, device_id={"space": partner}, device_id_type=MESH)

        @pl.when(reaches)
        def _():
            pl.semaphore_signal(barrier, inc=1, device_id={"space": diagonal}, device_id_type=MESH)

    @pl.when(core == 1)
    def _():
        pltpu.make_async_copy(forward, fwd, local_sem.at[0]).start()
        pltpu.make_async_copy(inverse, inv, local_sem.at[1]).start()

    pl.semaphore_wait(
        barrier,
        n_energy // 2 + jnp.where(reaches, core, 0),
    )

    hold.wait()

    def give(to):
        pltpu.make_async_remote_copy(
            src_ref=part(held, to),
            dst_ref=part(gathered, e),
            send_sem=gather_send,
            recv_sem=gather_sem,
            device_id={"energy": 2 * to + 1},
            device_id_type=MESH,
        ).start()

    for d in far:
        for across in (1, 0):
            give(2 * at_distance(d) + (1 - x if across else x))
    give(2 * y + 1 - x)

    @pl.when(core == 0)
    def _():
        give(mine)

    @pl.when(jnp.logical_not(reaches))
    def _():
        polar[2] = jnp.zeros(polar.shape[1:], BF16)

    def stage(y_from, y_to):
        block = 4 * rows
        return pltpu.make_async_remote_copy(
            src_ref=spectra.at[:, :, pl.ds(pl.multiple_of(y_to * block, block), block), :],
            dst_ref=staged.at[y_from],
            send_sem=stage_send,
            recv_sem=stage_sem.at[y_from],
            device_id={"energy": device(y_to, x, 1)},
            device_id_type=MESH,
        )

    def pass_on(y_from, piece):
        index = 2 * y_from + x

        def give_to(slot, row, send, recv):
            for across in (0, 1):
                for c in (0, 1):
                    x_to = 1 - x if across else x
                    pltpu.make_async_remote_copy(
                        src_ref=piece(2 * x_to + c),
                        dst_ref=part(polar.at[slot], index),
                        send_sem=send,
                        recv_sem=recv,
                        device_id={"energy": device(y, x_to, c), "space": row},
                        device_id_type=MESH,
                    ).start()

        @pl.when(reaches)
        def _():
            give_to(2, diagonal, z_send, z_sem)

        give_to(1, partner, x_send, x_sem)

    def hand_out(y_from, piece):
        index = 2 * y_from + x
        for across, c in ((1, 0), (1, 1), (0, 0)):
            x_to = 1 - x if across else x
            pltpu.make_async_remote_copy(
                src_ref=piece(2 * x_to + c),
                dst_ref=part(polar.at[0], index),
                send_sem=own_send,
                recv_sem=own_sem,
                device_id={"energy": device(y, x_to, c)},
                device_id_type=MESH,
            ).start()
        pltpu.make_async_copy(piece(2 * x + 1), part(polar.at[0], index), local_sem.at[2]).start()

    @pl.when(core == 1)
    def _():
        own = pltpu.make_async_copy(part(held, mine), part(gathered, e), local_sem.at[2])
        own.start()
        pltpu.make_async_copy(forward, fwd, local_sem.at[0]).wait()
        pltpu.make_async_copy(inverse, inv, local_sem.at[1]).wait()
        own.wait()
        others = gathered.at[:, :, pl.ds(0, (n_energy - 1) * rows), :]
        pltpu.make_async_copy(others, others, gather_sem).wait()
        pl.semaphore_signal(x_open, inc=1, device_id={"space": partner}, device_id_type=MESH)

        @pl.when(reaches)
        def _():
            pl.semaphore_signal(z_open, inc=1, device_id={"space": diagonal}, device_id_type=MESH)

        size = gathered.shape[-1]
        half = 2 * size
        stacked = jnp.concatenate(
            [
                jnp.concatenate([gathered[2 * a, h], gathered[2 * a + 1, h]], axis=0)
                for a in range(2)
                for h in range(2)
            ],
            axis=1,
        )
        real_parts, imag_parts = [], []
        step = half // 2
        for c in range(2):
            real = jnp.dot(fwd[c * step:(c + 1) * step], stacked, preferred_element_type=jnp.float32)
            imag = jnp.dot(fwd[half + c * step:half + (c + 1) * step], stacked, preferred_element_type=jnp.float32)
            less_re, less_im = real[:, :half], imag[:, :half]
            great_re, great_im = real[:, half:], imag[:, half:]
            real_parts.append((less_re * great_im - less_im * great_re).astype(BF16))
            imag_parts.append((less_re * great_re + less_im * great_im).astype(BF16))
        product = jnp.concatenate(real_parts + imag_parts, axis=0)
        result = jnp.dot(inv[...], product, preferred_element_type=jnp.float32).astype(BF16)
        for i in range(4):
            for h in range(2):
                spectra[i, h] = result[i * size:(i + 1) * size, h * size:(h + 1) * size]

        for d in (1, -1, 2, -2, 4, 3, -3):
            stage(y, at_distance(d)).start()
        pl.semaphore_wait(x_open, 1)

        @pl.when(reaches)
        def _():
            pl.semaphore_wait(z_open, 1)

        pieces = [(y, lambda j: part(spectra, 4 * y + j))]
        for d in near:
            y_from = at_distance(d)
            pieces.append((y_from, lambda j, y_from=y_from: staged.at[y_from, :, :, pl.ds(j * rows, rows), :]))
        for i, (y_from, piece) in enumerate(pieces):
            if i > 0:
                stage(y_from, y_from).wait_recv()
            hand_out(y_from, piece)
            pass_on(y_from, piece)
        for y_from, piece in pieces[KEEP:]:
            hand_out(y_from, piece)

    half_own = polar.at[0, pl.ds(0, 2)]

    @pl.when(core == 0)
    def _():
        pltpu.make_async_copy(polar.at[0], polar.at[0], own_sem).wait()

    @pl.when(core == 1)
    def _():
        pltpu.make_async_copy(half_own, half_own, own_sem).wait()
        pltpu.make_async_copy(half_own, half_own, local_sem.at[2]).wait()

    sent = gathered.at[:, :, pl.ds(0, (n_energy // 2 - 1) * rows), :]
    pltpu.make_async_copy(sent, sent, gather_send).wait()

    @pl.when(core == 0)
    def _():
        one = part(polar.at[0], 0)
        pltpu.make_async_copy(one, one, gather_send).wait()

    @pl.when(core == 1)
    def _():
        back = spectra.at[:, :, pl.ds(0, (n_y - 1) * 4 * rows), :]
        pltpu.make_async_copy(back, back, stage_send).wait()
        six = staged.at[pl.ds(0, 6)]
        pltpu.make_async_copy(six, six, own_send).wait()
        pltpu.make_async_copy(staged, staged, x_send).wait()

        @pl.when(reaches)
        def _():
            pltpu.make_async_copy(staged, staged, z_send).wait()

    pltpu.make_async_copy(polar.at[1], polar.at[1], x_sem).wait()

    @pl.when(reaches)
    def _():
        pltpu.make_async_copy(polar.at[2], polar.at[2], z_sem).wait()


def product_kernel(n_space, polar, coulomb, pattern, sides, screened, out_sides, out_screened, out_sem):
    size = coulomb.shape[-1]
    s = lax.axis_index("space")
    high = s % 2

    present = pattern[...].astype(jnp.float32)
    below = present[:, 0:1] * jnp.where(s > 0, 1.0, 0.0)
    above = present[:, 1:2] * jnp.where(s < n_space - 1, 1.0, 0.0)

    def coupling(upper):
        mark = jnp.where(upper == 1, above, below)
        return (coulomb[2 * upper].astype(jnp.float32) * mark).astype(BF16)

    def image(weight, slot):
        wide = jnp.concatenate([polar[slot, i].reshape(size, size) for i in range(4)], axis=1)
        return jnp.dot(weight, wide, preferred_element_type=jnp.float32).astype(BF16)

    weights = (coulomb[1], coupling(1 - high), coupling(high))
    copies = []
    images = [image(weights[0], 0)]
    for slot, block in ((1, 1 - high), (2, high)):
        images.append(image(weights[slot], slot))
        for i in range(4):
            out_sides[slot - 1, i // 2, i % 2] = images[slot][:, i * size:(i + 1) * size]
        copies.append(pltpu.make_async_copy(out_sides.at[slot - 1], sides.at[:, block], out_sem.at[slot - 1]))
    joined = jnp.concatenate(
        [jnp.concatenate([part[:, i * size:(i + 1) * size] for part in images], axis=1) for i in range(4)], axis=0
    )
    result = lax.dot_general(
        joined,
        jnp.concatenate(weights, axis=1),
        (((1,), (1,)), ((), ())),
        preferred_element_type=jnp.float32,
    ).astype(BF16)
    for i in range(4):
        out_screened[i] = result[i * size:(i + 1) * size]
    last = pltpu.make_async_copy(out_screened, screened, out_sem.at[2])
    for copy in copies:
        copy.start()
    last.start()
    for copy in copies:
        copy.wait()
    last.wait()


def solution(mesh):
    n_energy, n_space = mesh.shape["energy"], mesh.shape["space"]

    def local(greens, coulomb, pattern):
        size = greens.shape[-1]
        rows = size // n_energy
        forward, inverse = make_tables(n_energy, rows)
        anywhere = pl.BlockSpec(memory_space=pl.ANY)
        vmem = pl.BlockSpec(memory_space=pltpu.VMEM)
        dma = pltpu.SemaphoreType.DMA
        strips = n_energy // 4
        polar = pl.pallas_call(
            lambda *refs: exchange_kernel(n_energy, n_space, rows, *refs),
            out_shape=pltpu.VMEM((3, 4, 2, size // 2, size), BF16),
            in_specs=[anywhere] * 3,
            out_specs=vmem,
            scratch_shapes=[
                pltpu.VMEM((4, 2, size, size), BF16),
                pltpu.VMEM((4, 2, size, size), BF16),
                pltpu.VMEM((strips, 4, 2, 4 * rows, size), BF16),
                pltpu.VMEM(forward.shape, BF16),
                pltpu.VMEM(inverse.shape, BF16),
                pltpu.VMEM((4, 2, size // 2, size), BF16),
                dma, dma, dma, dma((strips,)), dma, dma, dma, dma, dma, dma, dma((4,)),
                pltpu.SemaphoreType.REGULAR, pltpu.SemaphoreType.REGULAR,
            ],
            compiler_params=pltpu.CompilerParams(collective_id=0, has_side_effects=True),
            name="exchange",
        )(greens.reshape(4, 2, size // 2, size), jnp.asarray(forward), jnp.asarray(inverse))
        sides, screened = pl.pallas_call(
            lambda *refs: product_kernel(n_space, *refs),
            out_shape=(
                jax.ShapeDtypeStruct((2, 2, 2, size, size), BF16),
                jax.ShapeDtypeStruct((4, size, size), BF16),
            ),
            in_specs=[vmem, vmem, vmem],
            out_specs=(anywhere, anywhere),
            scratch_shapes=[
                pltpu.VMEM((2, 2, 2, size, size), BF16),
                pltpu.VMEM((4, size, size), BF16),
                dma((3,)),
            ],
            compiler_params=pltpu.CompilerParams(vmem_limit_bytes=16 << 20),
            name="products",
        )(polar, coulomb.reshape(3, size, size), pattern)
        return sides.reshape(2, 2, 2, 1, size, size), screened.reshape(2, 2, 1, size, size)

    return jax.shard_map(
        local,
        mesh=mesh,
        in_specs=(P(None, None, "energy", "space", None), P(None, "space", None), P("space", None)),
        out_specs=(P(None, None, None, "energy", "space", None), P(None, None, "energy", "space", None)),
        check_vma=False,
    )
```

```python
import math

import jax
import jax.numpy as jnp
import numpy as np
from jax import lax
from jax.experimental import pallas as pl
from jax.experimental.pallas import tpu as pltpu
from jax.sharding import PartitionSpec as P

MESH = pl.DeviceIdType.MESH
BF16 = jnp.bfloat16


def make_tables(energies, rows):
    period = 2 * energies
    phases = (np.arange(period)[:, None] * np.arange(energies)[None, :] % period) * (2.0 * math.pi / period)
    cos_part, sin_part = np.cos(phases), np.sin(phases)
    forward = np.block([[cos_part, sin_part], [-sin_part, cos_part]])
    cos_back, sin_back = cos_part.T, sin_part.T
    inverse = np.block(
        [[cos_back, -sin_back], [sin_back, cos_back], [-cos_back, -sin_back], [-sin_back, cos_back]]
    ) * (1.0 / (period * math.sqrt(energies)))
    unit = np.eye(rows)
    return tuple(np.kron(table, unit).astype(np.float32).astype(BF16) for table in (forward, inverse))


def exchange_kernel(
    n_energy, n_space, rows,
    greens, forward, inverse,
    polar,
    gathered, spectra, staged, fwd, inv, held,
    gather_send, gather_sem, stage_send, stage_sem, own_send, own_sem, x_send, x_sem, z_send, z_sem, local_sem, x_open, z_open,
):
    e = lax.axis_index("energy")
    s = lax.axis_index("space")
    n_y = n_energy // 4
    core, mine, y = lax.rem(e, 2), lax.div(e, 2), lax.div(e, 4)
    x = mine - 2 * y
    z = lax.div(s, 2)
    high = s - 2 * z
    n_z = n_space // 2
    partner = s + 1 - 2 * high
    diagonal = s - 1 + 2 * high
    reaches = jnp.where(high == 0, z > 0, z < n_z - 1)
    near = []
    for d in range(1, n_y // 2):
        near += [d, -d]
    near.append(n_y // 2)
    far = near[::-1]

    def part(ref, index):
        return ref.at[:, :, pl.ds(pl.multiple_of(index * rows, rows), rows), :]

    def at_distance(d):
        return lax.rem(y + (d + n_y) % n_y, n_y)

    def device(y_to, x_to, core_to):
        return 4 * y_to + 2 * x_to + core_to

    hold = pltpu.make_async_copy(greens, held, local_sem.at[3])
    hold.start()
    barrier = pltpu.get_barrier_semaphore()

    @pl.when(core == 1)
    def _():
        def greet(to):
            pl.semaphore_signal(barrier, inc=1, device_id={"energy": to}, device_id_type=MESH)

        for d in far:
            for x_to in range(2):
                for c in range(2):
                    greet(device(at_distance(d), x_to, c))
        greet(device(y, 1 - x, 0))
        greet(device(y, 1 - x, 1))
        greet(e - 1)
        pl.semaphore_signal(barrier, inc=1, device_id={"space": partner}, device_id_type=MESH)

        @pl.when(reaches)
        def _():
            pl.semaphore_signal(barrier, inc=1, device_id={"space": diagonal}, device_id_type=MESH)

    @pl.when(core == 1)
    def _():
        pltpu.make_async_copy(forward, fwd, local_sem.at[0]).start()
        pltpu.make_async_copy(inverse, inv, local_sem.at[1]).start()

    pl.semaphore_wait(
        barrier,
        n_energy // 2 + jnp.where(reaches, core, 0),
    )

    hold.wait()

    def give(to):
        pltpu.make_async_remote_copy(
            src_ref=part(held, to),
            dst_ref=part(gathered, e),
            send_sem=gather_send,
            recv_sem=gather_sem,
            device_id={"energy": 2 * to + 1},
            device_id_type=MESH,
        ).start()

    for d in far:
        for across in (1, 0):
            give(2 * at_distance(d) + (1 - x if across else x))
    give(2 * y + 1 - x)

    @pl.when(core == 0)
    def _():
        give(mine)

    @pl.when(jnp.logical_not(reaches))
    def _():
        polar[2] = jnp.zeros(polar.shape[1:], BF16)

    def stage(y_from, y_to):
        block = 4 * rows
        return pltpu.make_async_remote_copy(
            src_ref=spectra.at[:, :, pl.ds(pl.multiple_of(y_to * block, block), block), :],
            dst_ref=staged.at[y_from],
            send_sem=stage_send,
            recv_sem=stage_sem.at[y_from],
            device_id={"energy": device(y_to, x, 1)},
            device_id_type=MESH,
        )

    def pass_on(y_from, piece):
        index = 2 * y_from + x

        def give_to(slot, row, send, recv):
            for across in (0, 1):
                for c in (0, 1):
                    x_to = 1 - x if across else x
                    pltpu.make_async_remote_copy(
                        src_ref=piece(2 * x_to + c),
                        dst_ref=part(polar.at[slot], index),
                        send_sem=send,
                        recv_sem=recv,
                        device_id={"energy": device(y, x_to, c), "space": row},
                        device_id_type=MESH,
                    ).start()

        @pl.when(reaches)
        def _():
            give_to(2, diagonal, z_send, z_sem)

        give_to(1, partner, x_send, x_sem)

    def hand_out(y_from, piece):
        index = 2 * y_from + x
        for across, c in ((1, 0), (1, 1), (0, 0)):
            x_to = 1 - x if across else x
            pltpu.make_async_remote_copy(
                src_ref=piece(2 * x_to + c),
                dst_ref=part(polar.at[0], index),
                send_sem=own_send,
                recv_sem=own_sem,
                device_id={"energy": device(y, x_to, c)},
                device_id_type=MESH,
            ).start()
        pltpu.make_async_copy(piece(2 * x + 1), part(polar.at[0], index), local_sem.at[2]).start()

    @pl.when(core == 1)
    def _():
        own = pltpu.make_async_copy(part(held, mine), part(gathered, e), local_sem.at[2])
        own.start()
        pltpu.make_async_copy(forward, fwd, local_sem.at[0]).wait()
        pltpu.make_async_copy(inverse, inv, local_sem.at[1]).wait()
        own.wait()
        others = gathered.at[:, :, pl.ds(0, (n_energy - 1) * rows), :]
        pltpu.make_async_copy(others, others, gather_sem).wait()
        pl.semaphore_signal(x_open, inc=1, device_id={"space": partner}, device_id_type=MESH)

        @pl.when(reaches)
        def _():
            pl.semaphore_signal(z_open, inc=1, device_id={"space": diagonal}, device_id_type=MESH)

        size = gathered.shape[-1]
        half = 2 * size
        stacked = jnp.concatenate(
            [
                jnp.concatenate([gathered[2 * a, h], gathered[2 * a + 1, h]], axis=0)
                for a in range(2)
                for h in range(2)
            ],
            axis=1,
        )
        real_parts, imag_parts = [], []
        step = half // 2
        for c in range(2):
            real = jnp.dot(fwd[c * step:(c + 1) * step], stacked, preferred_element_type=jnp.float32)
            imag = jnp.dot(fwd[half + c * step:half + (c + 1) * step], stacked, preferred_element_type=jnp.float32)
            less_re, less_im = real[:, :half], imag[:, :half]
            great_re, great_im = real[:, half:], imag[:, half:]
            real_parts.append((less_re * great_im - less_im * great_re).astype(BF16))
            imag_parts.append((less_re * great_re + less_im * great_im).astype(BF16))
        product = jnp.concatenate(real_parts + imag_parts, axis=0)
        result = jnp.dot(inv[...], product, preferred_element_type=jnp.float32).astype(BF16)
        for i in range(4):
            for h in range(2):
                spectra[i, h] = result[i * size:(i + 1) * size, h * size:(h + 1) * size]

        for d in (1, -1, 2, -2, 4, 3, -3):
            stage(y, at_distance(d)).start()
        pieces = [(y, lambda j: part(spectra, 4 * y + j))]
        for d in near:
            y_from = at_distance(d)
            pieces.append((y_from, lambda j, y_from=y_from: staged.at[y_from, :, :, pl.ds(j * rows, rows), :]))
        for i, (y_from, piece) in enumerate(pieces):
            if i > 0:
                stage(y_from, y_from).wait_recv()
            hand_out(y_from, piece)
            if i == 0:
                pl.semaphore_wait(x_open, 1)

                @pl.when(reaches)
                def _():
                    pl.semaphore_wait(z_open, 1)

            pass_on(y_from, piece)

    half_own = polar.at[0, pl.ds(0, 2)]

    @pl.when(core == 0)
    def _():
        pltpu.make_async_copy(polar.at[0], polar.at[0], own_sem).wait()

    @pl.when(core == 1)
    def _():
        pltpu.make_async_copy(half_own, half_own, own_sem).wait()
        pltpu.make_async_copy(half_own, half_own, local_sem.at[2]).wait()

    sent = gathered.at[:, :, pl.ds(0, (n_energy // 2 - 1) * rows), :]
    pltpu.make_async_copy(sent, sent, gather_send).wait()

    @pl.when(core == 0)
    def _():
        one = part(polar.at[0], 0)
        pltpu.make_async_copy(one, one, gather_send).wait()

    @pl.when(core == 1)
    def _():
        back = spectra.at[:, :, pl.ds(0, (n_y - 1) * 4 * rows), :]
        pltpu.make_async_copy(back, back, stage_send).wait()
        six = staged.at[pl.ds(0, 6)]
        pltpu.make_async_copy(six, six, own_send).wait()
        pltpu.make_async_copy(staged, staged, x_send).wait()

        @pl.when(reaches)
        def _():
            pltpu.make_async_copy(staged, staged, z_send).wait()

    pltpu.make_async_copy(polar.at[1], polar.at[1], x_sem).wait()

    @pl.when(reaches)
    def _():
        pltpu.make_async_copy(polar.at[2], polar.at[2], z_sem).wait()


def product_kernel(n_space, polar, coulomb, pattern, sides, screened, out_sides, out_screened, out_sem):
    size = coulomb.shape[-1]
    s = lax.axis_index("space")
    high = s % 2

    present = pattern[...].astype(jnp.float32)
    below = present[:, 0:1] * jnp.where(s > 0, 1.0, 0.0)
    above = present[:, 1:2] * jnp.where(s < n_space - 1, 1.0, 0.0)

    def coupling(upper):
        mark = jnp.where(upper == 1, above, below)
        return (coulomb[2 * upper].astype(jnp.float32) * mark).astype(BF16)

    def image(weight, slot):
        wide = jnp.concatenate([polar[slot, i].reshape(size, size) for i in range(4)], axis=1)
        return jnp.dot(weight, wide, preferred_element_type=jnp.float32).astype(BF16)

    weights = (coulomb[1], coupling(1 - high), coupling(high))
    copies = []
    images = [image(weights[0], 0)]
    for slot, block in ((1, 1 - high), (2, high)):
        images.append(image(weights[slot], slot))
        for i in range(4):
            out_sides[slot - 1, i // 2, i % 2] = images[slot][:, i * size:(i + 1) * size]
        copies.append(pltpu.make_async_copy(out_sides.at[slot - 1], sides.at[:, block], out_sem.at[slot - 1]))
    joined = jnp.concatenate(
        [jnp.concatenate([part[:, i * size:(i + 1) * size] for part in images], axis=1) for i in range(4)], axis=0
    )
    result = lax.dot_general(
        joined,
        jnp.concatenate(weights, axis=1),
        (((1,), (1,)), ((), ())),
        preferred_element_type=jnp.float32,
    ).astype(BF16)
    for i in range(4):
        out_screened[i] = result[i * size:(i + 1) * size]
    last = pltpu.make_async_copy(out_screened, screened, out_sem.at[2])
    for copy in copies:
        copy.start()
    last.start()
    for copy in copies:
        copy.wait()
    last.wait()


def solution(mesh):
    n_energy, n_space = mesh.shape["energy"], mesh.shape["space"]

    def local(greens, coulomb, pattern):
        size = greens.shape[-1]
        rows = size // n_energy
        forward, inverse = make_tables(n_energy, rows)
        anywhere = pl.BlockSpec(memory_space=pl.ANY)
        vmem = pl.BlockSpec(memory_space=pltpu.VMEM)
        dma = pltpu.SemaphoreType.DMA
        strips = n_energy // 4
        polar = pl.pallas_call(
            lambda *refs: exchange_kernel(n_energy, n_space, rows, *refs),
            out_shape=pltpu.VMEM((3, 4, 2, size // 2, size), BF16),
            in_specs=[anywhere] * 3,
            out_specs=vmem,
            scratch_shapes=[
                pltpu.VMEM((4, 2, size, size), BF16),
                pltpu.VMEM((4, 2, size, size), BF16),
                pltpu.VMEM((strips, 4, 2, 4 * rows, size), BF16),
                pltpu.VMEM(forward.shape, BF16),
                pltpu.VMEM(inverse.shape, BF16),
                pltpu.VMEM((4, 2, size // 2, size), BF16),
                dma, dma, dma, dma((strips,)), dma, dma, dma, dma, dma, dma, dma((4,)),
                pltpu.SemaphoreType.REGULAR, pltpu.SemaphoreType.REGULAR,
            ],
            compiler_params=pltpu.CompilerParams(collective_id=0, has_side_effects=True),
            name="exchange",
        )(greens.reshape(4, 2, size // 2, size), jnp.asarray(forward), jnp.asarray(inverse))
        sides, screened = pl.pallas_call(
            lambda *refs: product_kernel(n_space, *refs),
            out_shape=(
                jax.ShapeDtypeStruct((2, 2, 2, size, size), BF16),
                jax.ShapeDtypeStruct((4, size, size), BF16),
            ),
            in_specs=[vmem, vmem, vmem],
            out_specs=(anywhere, anywhere),
            scratch_shapes=[
                pltpu.VMEM((2, 2, 2, size, size), BF16),
                pltpu.VMEM((4, size, size), BF16),
                dma((3,)),
            ],
            compiler_params=pltpu.CompilerParams(vmem_limit_bytes=16 << 20),
            name="products",
        )(polar, coulomb.reshape(3, size, size), pattern)
        return sides.reshape(2, 2, 2, 1, size, size), screened.reshape(2, 2, 1, size, size)

    return jax.shard_map(
        local,
        mesh=mesh,
        in_specs=(P(None, None, "energy", "space", None), P(None, "space", None), P("space", None)),
        out_specs=(P(None, None, None, "energy", "space", None), P(None, None, "energy", "space", None)),
        check_vma=False,
    )
```

```python
import math

import jax
import jax.numpy as jnp
import numpy as np
from jax import lax
from jax.experimental import pallas as pl
from jax.experimental.pallas import tpu as pltpu
from jax.sharding import PartitionSpec as P

MESH = pl.DeviceIdType.MESH
BF16 = jnp.bfloat16
KEEP = 8


def make_tables(energies, rows):
    period = 2 * energies
    phases = (np.arange(period)[:, None] * np.arange(energies)[None, :] % period) * (2.0 * math.pi / period)
    cos_part, sin_part = np.cos(phases), np.sin(phases)
    forward = np.block([[cos_part, sin_part], [-sin_part, cos_part]])
    cos_back, sin_back = cos_part.T, sin_part.T
    inverse = np.block(
        [[cos_back, -sin_back], [sin_back, cos_back], [-cos_back, -sin_back], [-sin_back, cos_back]]
    ) * (1.0 / (period * math.sqrt(energies)))
    unit = np.eye(rows)
    return tuple(np.kron(table, unit).astype(np.float32).astype(BF16) for table in (forward, inverse))


def exchange_kernel(
    n_energy, n_space, rows,
    greens, forward, inverse,
    polar,
    gathered, spectra, staged, fwd, inv, held,
    gather_send, gather_sem, stage_send, stage_sem, own_send, own_sem, x_send, x_sem, z_send, z_sem, local_sem, x_open, z_open,
):
    e = lax.axis_index("energy")
    s = lax.axis_index("space")
    n_y = n_energy // 4
    core, mine, y = lax.rem(e, 2), lax.div(e, 2), lax.div(e, 4)
    x = mine - 2 * y
    z = lax.div(s, 2)
    high = s - 2 * z
    n_z = n_space // 2
    partner = s + 1 - 2 * high
    diagonal = s - 1 + 2 * high
    reaches = jnp.where(high == 0, z > 0, z < n_z - 1)
    near = []
    for d in range(1, n_y // 2):
        near += [d, -d]
    near.append(n_y // 2)
    far = near[::-1]

    def part(ref, index):
        return ref.at[:, :, pl.ds(pl.multiple_of(index * rows, rows), rows), :]

    def at_distance(d):
        return lax.rem(y + (d + n_y) % n_y, n_y)

    def device(y_to, x_to, core_to):
        return 4 * y_to + 2 * x_to + core_to

    hold = pltpu.make_async_copy(greens, held, local_sem.at[3])
    hold.start()
    barrier = pltpu.get_barrier_semaphore()

    @pl.when(core == 1)
    def _():
        def greet(to):
            pl.semaphore_signal(barrier, inc=1, device_id={"energy": to}, device_id_type=MESH)

        for d in far:
            for x_to in range(2):
                for c in range(2):
                    greet(device(at_distance(d), x_to, c))
        greet(device(y, 1 - x, 0))
        greet(device(y, 1 - x, 1))
        greet(e - 1)
        pl.semaphore_signal(barrier, inc=1, device_id={"space": partner}, device_id_type=MESH)

        @pl.when(reaches)
        def _():
            pl.semaphore_signal(barrier, inc=1, device_id={"space": diagonal}, device_id_type=MESH)

    @pl.when(core == 1)
    def _():
        pltpu.make_async_copy(forward, fwd, local_sem.at[0]).start()
        pltpu.make_async_copy(inverse, inv, local_sem.at[1]).start()

    pl.semaphore_wait(
        barrier,
        n_energy // 2 + jnp.where(reaches, core, 0),
    )

    hold.wait()

    def give(to):
        pltpu.make_async_remote_copy(
            src_ref=part(held, to),
            dst_ref=part(gathered, e),
            send_sem=gather_send,
            recv_sem=gather_sem,
            device_id={"energy": 2 * to + 1},
            device_id_type=MESH,
        ).start()

    for d in far:
        for across in (1, 0):
            give(2 * at_distance(d) + (1 - x if across else x))
    give(2 * y + 1 - x)

    @pl.when(core == 0)
    def _():
        give(mine)

    @pl.when(jnp.logical_not(reaches))
    def _():
        polar[2] = jnp.zeros(polar.shape[1:], BF16)

    def stage(y_from, y_to):
        block = 4 * rows
        return pltpu.make_async_remote_copy(
            src_ref=spectra.at[:, :, pl.ds(pl.multiple_of(y_to * block, block), block), :],
            dst_ref=staged.at[y_from],
            send_sem=stage_send,
            recv_sem=stage_sem.at[y_from],
            device_id={"energy": device(y_to, x, 1)},
            device_id_type=MESH,
        )

    def pass_on(y_from, piece):
        index = 2 * y_from + x

        def give_to(slot, row, send, recv):
            for across in (0, 1):
                for c in (0, 1):
                    x_to = 1 - x if across else x
                    pltpu.make_async_remote_copy(
                        src_ref=piece(2 * x_to + c),
                        dst_ref=part(polar.at[slot], index),
                        send_sem=send,
                        recv_sem=recv,
                        device_id={"energy": device(y, x_to, c), "space": row},
                        device_id_type=MESH,
                    ).start()

        give_to(1, partner, x_send, x_sem)

        @pl.when(reaches)
        def _():
            give_to(2, diagonal, z_send, z_sem)

    def hand_out(y_from, piece):
        index = 2 * y_from + x
        for across, c in ((1, 0), (1, 1), (0, 0)):
            x_to = 1 - x if across else x
            pltpu.make_async_remote_copy(
                src_ref=piece(2 * x_to + c),
                dst_ref=part(polar.at[0], index),
                send_sem=own_send,
                recv_sem=own_sem,
                device_id={"energy": device(y, x_to, c)},
                device_id_type=MESH,
            ).start()
        pltpu.make_async_copy(piece(2 * x + 1), part(polar.at[0], index), local_sem.at[2]).start()

    @pl.when(core == 1)
    def _():
        own = pltpu.make_async_copy(part(held, mine), part(gathered, e), local_sem.at[2])
        own.start()
        pltpu.make_async_copy(forward, fwd, local_sem.at[0]).wait()
        pltpu.make_async_copy(inverse, inv, local_sem.at[1]).wait()
        own.wait()
        others = gathered.at[:, :, pl.ds(0, (n_energy - 1) * rows), :]
        pltpu.make_async_copy(others, others, gather_sem).wait()
        pl.semaphore_signal(x_open, inc=1, device_id={"space": partner}, device_id_type=MESH)

        @pl.when(reaches)
        def _():
            pl.semaphore_signal(z_open, inc=1, device_id={"space": diagonal}, device_id_type=MESH)

        size = gathered.shape[-1]
        half = 2 * size
        stacked = jnp.concatenate(
            [
                jnp.concatenate([gathered[2 * a, h], gathered[2 * a + 1, h]], axis=0)
                for a in range(2)
                for h in range(2)
            ],
            axis=1,
        )
        real_parts, imag_parts = [], []
        step = half // 2
        for c in range(2):
            real = jnp.dot(fwd[c * step:(c + 1) * step], stacked, preferred_element_type=jnp.float32)
            imag = jnp.dot(fwd[half + c * step:half + (c + 1) * step], stacked, preferred_element_type=jnp.float32)
            less_re, less_im = real[:, :half], imag[:, :half]
            great_re, great_im = real[:, half:], imag[:, half:]
            real_parts.append((less_re * great_im - less_im * great_re).astype(BF16))
            imag_parts.append((less_re * great_re + less_im * great_im).astype(BF16))
        product = jnp.concatenate(real_parts + imag_parts, axis=0)
        result = jnp.dot(inv[...], product, preferred_element_type=jnp.float32).astype(BF16)
        for i in range(4):
            for h in range(2):
                spectra[i, h] = result[i * size:(i + 1) * size, h * size:(h + 1) * size]

        for d in (1, -1, 2, -2, 4, 3, -3):
            stage(y, at_distance(d)).start()
        pl.semaphore_wait(x_open, 1)

        @pl.when(reaches)
        def _():
            pl.semaphore_wait(z_open, 1)

        pieces = [(y, lambda j: part(spectra, 4 * y + j))]
        for d in near:
            y_from = at_distance(d)
            pieces.append((y_from, lambda j, y_from=y_from: staged.at[y_from, :, :, pl.ds(j * rows, rows), :]))
        for i, (y_from, piece) in enumerate(pieces):
            if i > 0:
                stage(y_from, y_from).wait_recv()
            hand_out(y_from, piece)
            pass_on(y_from, piece)
        for y_from, piece in pieces[KEEP:]:
            hand_out(y_from, piece)

    half_own = polar.at[0, pl.ds(0, 2)]

    @pl.when(core == 0)
    def _():
        pltpu.make_async_copy(polar.at[0], polar.at[0], own_sem).wait()

    @pl.when(core == 1)
    def _():
        pltpu.make_async_copy(half_own, half_own, own_sem).wait()
        pltpu.make_async_copy(half_own, half_own, local_sem.at[2]).wait()

    sent = gathered.at[:, :, pl.ds(0, (n_energy // 2 - 1) * rows), :]
    pltpu.make_async_copy(sent, sent, gather_send).wait()

    @pl.when(core == 0)
    def _():
        one = part(polar.at[0], 0)
        pltpu.make_async_copy(one, one, gather_send).wait()

    @pl.when(core == 1)
    def _():
        back = spectra.at[:, :, pl.ds(0, (n_y - 1) * 4 * rows), :]
        pltpu.make_async_copy(back, back, stage_send).wait()
        six = staged.at[pl.ds(0, 6)]
        pltpu.make_async_copy(six, six, own_send).wait()
        pltpu.make_async_copy(staged, staged, x_send).wait()

        @pl.when(reaches)
        def _():
            pltpu.make_async_copy(staged, staged, z_send).wait()

    pltpu.make_async_copy(polar.at[1], polar.at[1], x_sem).wait()

    @pl.when(reaches)
    def _():
        pltpu.make_async_copy(polar.at[2], polar.at[2], z_sem).wait()


def product_kernel(n_space, polar, coulomb, pattern, sides, screened, out_sides, out_screened, out_sem):
    size = coulomb.shape[-1]
    s = lax.axis_index("space")
    high = s % 2

    present = pattern[...].astype(jnp.float32)
    below = present[:, 0:1] * jnp.where(s > 0, 1.0, 0.0)
    above = present[:, 1:2] * jnp.where(s < n_space - 1, 1.0, 0.0)

    def coupling(upper):
        mark = jnp.where(upper == 1, above, below)
        return (coulomb[2 * upper].astype(jnp.float32) * mark).astype(BF16)

    def image(weight, slot):
        wide = jnp.concatenate([polar[slot, i].reshape(size, size) for i in range(4)], axis=1)
        return jnp.dot(weight, wide, preferred_element_type=jnp.float32).astype(BF16)

    weights = (coulomb[1], coupling(1 - high), coupling(high))
    copies = []
    images = [image(weights[0], 0)]
    for slot, block in ((1, 1 - high), (2, high)):
        images.append(image(weights[slot], slot))
        for i in range(4):
            out_sides[slot - 1, i // 2, i % 2] = images[slot][:, i * size:(i + 1) * size]
        copies.append(pltpu.make_async_copy(out_sides.at[slot - 1], sides.at[:, block], out_sem.at[slot - 1]))
    joined = jnp.concatenate(
        [jnp.concatenate([part[:, i * size:(i + 1) * size] for part in images], axis=1) for i in range(4)], axis=0
    )
    result = lax.dot_general(
        joined,
        jnp.concatenate(weights, axis=1),
        (((1,), (1,)), ((), ())),
        preferred_element_type=jnp.float32,
    ).astype(BF16)
    for i in range(4):
        out_screened[i] = result[i * size:(i + 1) * size]
    last = pltpu.make_async_copy(out_screened, screened, out_sem.at[2])
    for copy in copies:
        copy.start()
    last.start()
    for copy in copies:
        copy.wait()
    last.wait()


def solution(mesh):
    n_energy, n_space = mesh.shape["energy"], mesh.shape["space"]

    def local(greens, coulomb, pattern):
        size = greens.shape[-1]
        rows = size // n_energy
        forward, inverse = make_tables(n_energy, rows)
        anywhere = pl.BlockSpec(memory_space=pl.ANY)
        vmem = pl.BlockSpec(memory_space=pltpu.VMEM)
        dma = pltpu.SemaphoreType.DMA
        strips = n_energy // 4
        polar = pl.pallas_call(
            lambda *refs: exchange_kernel(n_energy, n_space, rows, *refs),
            out_shape=pltpu.VMEM((3, 4, 2, size // 2, size), BF16),
            in_specs=[anywhere] * 3,
            out_specs=vmem,
            scratch_shapes=[
                pltpu.VMEM((4, 2, size, size), BF16),
                pltpu.VMEM((4, 2, size, size), BF16),
                pltpu.VMEM((strips, 4, 2, 4 * rows, size), BF16),
                pltpu.VMEM(forward.shape, BF16),
                pltpu.VMEM(inverse.shape, BF16),
                pltpu.VMEM((4, 2, size // 2, size), BF16),
                dma, dma, dma, dma((strips,)), dma, dma, dma, dma, dma, dma, dma((4,)),
                pltpu.SemaphoreType.REGULAR, pltpu.SemaphoreType.REGULAR,
            ],
            compiler_params=pltpu.CompilerParams(collective_id=0, has_side_effects=True),
            name="exchange",
        )(greens.reshape(4, 2, size // 2, size), jnp.asarray(forward), jnp.asarray(inverse))
        sides, screened = pl.pallas_call(
            lambda *refs: product_kernel(n_space, *refs),
            out_shape=(
                jax.ShapeDtypeStruct((2, 2, 2, size, size), BF16),
                jax.ShapeDtypeStruct((4, size, size), BF16),
            ),
            in_specs=[vmem, vmem, vmem],
            out_specs=(anywhere, anywhere),
            scratch_shapes=[
                pltpu.VMEM((2, 2, 2, size, size), BF16),
                pltpu.VMEM((4, size, size), BF16),
                dma((3,)),
            ],
            compiler_params=pltpu.CompilerParams(vmem_limit_bytes=16 << 20),
            name="products",
        )(polar, coulomb.reshape(3, size, size), pattern)
        return sides.reshape(2, 2, 2, 1, size, size), screened.reshape(2, 2, 1, size, size)

    return jax.shard_map(
        local,
        mesh=mesh,
        in_specs=(P(None, None, "energy", "space", None), P(None, "space", None), P("space", None)),
        out_specs=(P(None, None, None, "energy", "space", None), P(None, None, "energy", "space", None)),
        check_vma=False,
    )
```

```python
import math

import jax
import jax.numpy as jnp
import numpy as np
from jax import lax
from jax.experimental import pallas as pl
from jax.experimental.pallas import tpu as pltpu
from jax.sharding import PartitionSpec as P

MESH = pl.DeviceIdType.MESH
BF16 = jnp.bfloat16
KEEP = 8


def make_tables(energies, rows):
    period = 2 * energies
    phases = (np.arange(period)[:, None] * np.arange(energies)[None, :] % period) * (2.0 * math.pi / period)
    cos_part, sin_part = np.cos(phases), np.sin(phases)
    forward = np.block([[cos_part, sin_part], [-sin_part, cos_part]])
    cos_back, sin_back = cos_part.T, sin_part.T
    inverse = np.block(
        [[cos_back, -sin_back], [sin_back, cos_back], [-cos_back, -sin_back], [-sin_back, cos_back]]
    ) * (1.0 / (period * math.sqrt(energies)))
    unit = np.eye(rows)
    return tuple(np.kron(table, unit).astype(np.float32).astype(BF16) for table in (forward, inverse))


def exchange_kernel(
    n_energy, n_space, rows,
    greens, forward, inverse,
    polar,
    gathered, spectra, staged, fwd, inv, held,
    gather_send, gather_sem, stage_send, stage_sem, own_send, own_sem, x_send, x_sem, z_send, z_sem, local_sem, x_open, z_open,
):
    e = lax.axis_index("energy")
    s = lax.axis_index("space")
    n_y = n_energy // 4
    core, mine, y = lax.rem(e, 2), lax.div(e, 2), lax.div(e, 4)
    x = mine - 2 * y
    z = lax.div(s, 2)
    high = s - 2 * z
    n_z = n_space // 2
    partner = s + 1 - 2 * high
    diagonal = s - 1 + 2 * high
    reaches = jnp.where(high == 0, z > 0, z < n_z - 1)
    near = []
    for d in range(1, n_y // 2):
        near += [d, -d]
    near.append(n_y // 2)
    far = near[::-1]

    def part(ref, index):
        return ref.at[:, :, pl.ds(pl.multiple_of(index * rows, rows), rows), :]

    def at_distance(d):
        return lax.rem(y + (d + n_y) % n_y, n_y)

    def device(y_to, x_to, core_to):
        return 4 * y_to + 2 * x_to + core_to

    hold = pltpu.make_async_copy(greens, held, local_sem.at[3])
    hold.start()
    barrier = pltpu.get_barrier_semaphore()

    @pl.when(core == 1)
    def _():
        def greet(to):
            pl.semaphore_signal(barrier, inc=1, device_id={"energy": to}, device_id_type=MESH)

        for d in far:
            for x_to in range(2):
                for c in range(2):
                    greet(device(at_distance(d), x_to, c))
        greet(device(y, 1 - x, 0))
        greet(device(y, 1 - x, 1))
        greet(e - 1)
        pl.semaphore_signal(barrier, inc=1, device_id={"space": partner}, device_id_type=MESH)

        @pl.when(reaches)
        def _():
            pl.semaphore_signal(barrier, inc=1, device_id={"space": diagonal}, device_id_type=MESH)

    @pl.when(core == 1)
    def _():
        pltpu.make_async_copy(forward, fwd, local_sem.at[0]).start()
        pltpu.make_async_copy(inverse, inv, local_sem.at[1]).start()

    pl.semaphore_wait(
        barrier,
        n_energy // 2 + jnp.where(reaches, core, 0),
    )

    hold.wait()

    def give(to):
        pltpu.make_async_remote_copy(
            src_ref=part(held, to),
            dst_ref=part(gathered, e),
            send_sem=gather_send,
            recv_sem=gather_sem,
            device_id={"energy": 2 * to + 1},
            device_id_type=MESH,
        ).start()

    for d in far:
        for across in (1, 0):
            give(2 * at_distance(d) + (1 - x if across else x))
    give(2 * y + 1 - x)

    @pl.when(core == 0)
    def _():
        give(mine)

    @pl.when(jnp.logical_not(reaches))
    def _():
        polar[2] = jnp.zeros(polar.shape[1:], BF16)

    def stage(y_from, y_to):
        block = 4 * rows
        return pltpu.make_async_remote_copy(
            src_ref=spectra.at[:, :, pl.ds(pl.multiple_of(y_to * block, block), block), :],
            dst_ref=staged.at[y_from],
            send_sem=stage_send,
            recv_sem=stage_sem.at[y_from],
            device_id={"energy": device(y_to, x, 1)},
            device_id_type=MESH,
        )

    def pass_on(y_from, piece):
        index = 2 * y_from + x

        def give_to(slot, row, send, recv):
            for across in (0, 1):
                for c in (0, 1):
                    x_to = 1 - x if across else x
                    pltpu.make_async_remote_copy(
                        src_ref=piece(2 * x_to + c),
                        dst_ref=part(polar.at[slot], index),
                        send_sem=send,
                        recv_sem=recv,
                        device_id={"energy": device(y, x_to, c), "space": row},
                        device_id_type=MESH,
                    ).start()

        @pl.when(reaches)
        def _():
            give_to(2, diagonal, z_send, z_sem)

        give_to(1, partner, x_send, x_sem)

    def hand_out(y_from, piece):
        index = 2 * y_from + x
        for across, c in ((1, 0), (1, 1), (0, 0)):
            x_to = 1 - x if across else x
            pltpu.make_async_remote_copy(
                src_ref=piece(2 * x_to + c),
                dst_ref=part(polar.at[0], index),
                send_sem=own_send,
                recv_sem=own_sem,
                device_id={"energy": device(y, x_to, c)},
                device_id_type=MESH,
            ).start()
        pltpu.make_async_copy(piece(2 * x + 1), part(polar.at[0], index), local_sem.at[2]).start()

    @pl.when(core == 1)
    def _():
        own = pltpu.make_async_copy(part(held, mine), part(gathered, e), local_sem.at[2])
        own.start()
        pltpu.make_async_copy(forward, fwd, local_sem.at[0]).wait()
        pltpu.make_async_copy(inverse, inv, local_sem.at[1]).wait()
        own.wait()
        others = gathered.at[:, :, pl.ds(0, (n_energy - 1) * rows), :]
        pltpu.make_async_copy(others, others, gather_sem).wait()
        pl.semaphore_signal(x_open, inc=1, device_id={"space": partner}, device_id_type=MESH)

        @pl.when(reaches)
        def _():
            pl.semaphore_signal(z_open, inc=1, device_id={"space": diagonal}, device_id_type=MESH)

        size = gathered.shape[-1]
        half = 2 * size
        stacked = jnp.concatenate(
            [
                jnp.concatenate([gathered[2 * a, h], gathered[2 * a + 1, h]], axis=0)
                for a in range(2)
                for h in range(2)
            ],
            axis=1,
        )
        real_parts, imag_parts = [], []
        step = half // 4
        for c in range(4):
            real = jnp.dot(fwd[c * step:(c + 1) * step], stacked, preferred_element_type=jnp.float32)
            imag = jnp.dot(fwd[half + c * step:half + (c + 1) * step], stacked, preferred_element_type=jnp.float32)
            less_re, less_im = real[:, :half], imag[:, :half]
            great_re, great_im = real[:, half:], imag[:, half:]
            real_parts.append((less_re * great_im - less_im * great_re).astype(BF16))
            imag_parts.append((less_re * great_re + less_im * great_im).astype(BF16))
        product = jnp.concatenate(real_parts + imag_parts, axis=0)
        result = jnp.dot(inv[...], product, preferred_element_type=jnp.float32).astype(BF16)
        for i in range(4):
            for h in range(2):
                spectra[i, h] = result[i * size:(i + 1) * size, h * size:(h + 1) * size]

        for d in (1, -1, 2, -2, 4, 3, -3):
            stage(y, at_distance(d)).start()
        pl.semaphore_wait(x_open, 1)

        @pl.when(reaches)
        def _():
            pl.semaphore_wait(z_open, 1)

        pieces = [(y, lambda j: part(spectra, 4 * y + j))]
        for d in near:
            y_from = at_distance(d)
            pieces.append((y_from, lambda j, y_from=y_from: staged.at[y_from, :, :, pl.ds(j * rows, rows), :]))
        for i, (y_from, piece) in enumerate(pieces):
            if i > 0:
                stage(y_from, y_from).wait_recv()
            hand_out(y_from, piece)
            pass_on(y_from, piece)
        for y_from, piece in pieces[KEEP:]:
            hand_out(y_from, piece)

    half_own = polar.at[0, pl.ds(0, 2)]

    @pl.when(core == 0)
    def _():
        pltpu.make_async_copy(polar.at[0], polar.at[0], own_sem).wait()

    @pl.when(core == 1)
    def _():
        pltpu.make_async_copy(half_own, half_own, own_sem).wait()
        pltpu.make_async_copy(half_own, half_own, local_sem.at[2]).wait()

    sent = gathered.at[:, :, pl.ds(0, (n_energy // 2 - 1) * rows), :]
    pltpu.make_async_copy(sent, sent, gather_send).wait()

    @pl.when(core == 0)
    def _():
        one = part(polar.at[0], 0)
        pltpu.make_async_copy(one, one, gather_send).wait()

    @pl.when(core == 1)
    def _():
        back = spectra.at[:, :, pl.ds(0, (n_y - 1) * 4 * rows), :]
        pltpu.make_async_copy(back, back, stage_send).wait()
        six = staged.at[pl.ds(0, 6)]
        pltpu.make_async_copy(six, six, own_send).wait()
        pltpu.make_async_copy(staged, staged, x_send).wait()

        @pl.when(reaches)
        def _():
            pltpu.make_async_copy(staged, staged, z_send).wait()

    pltpu.make_async_copy(polar.at[1], polar.at[1], x_sem).wait()

    @pl.when(reaches)
    def _():
        pltpu.make_async_copy(polar.at[2], polar.at[2], z_sem).wait()


def product_kernel(n_space, polar, coulomb, pattern, sides, screened, out_sides, out_screened, out_sem):
    size = coulomb.shape[-1]
    s = lax.axis_index("space")
    high = s % 2

    present = pattern[...].astype(jnp.float32)
    below = present[:, 0:1] * jnp.where(s > 0, 1.0, 0.0)
    above = present[:, 1:2] * jnp.where(s < n_space - 1, 1.0, 0.0)

    def coupling(upper):
        mark = jnp.where(upper == 1, above, below)
        return (coulomb[2 * upper].astype(jnp.float32) * mark).astype(BF16)

    def image(weight, slot):
        wide = jnp.concatenate([polar[slot, i].reshape(size, size) for i in range(4)], axis=1)
        return jnp.dot(weight, wide, preferred_element_type=jnp.float32).astype(BF16)

    weights = (coulomb[1], coupling(1 - high), coupling(high))
    copies = []
    images = [image(weights[0], 0)]
    for slot, block in ((1, 1 - high), (2, high)):
        images.append(image(weights[slot], slot))
        for i in range(4):
            out_sides[slot - 1, i // 2, i % 2] = images[slot][:, i * size:(i + 1) * size]
        copies.append(pltpu.make_async_copy(out_sides.at[slot - 1], sides.at[:, block], out_sem.at[slot - 1]))
    joined = jnp.concatenate(
        [jnp.concatenate([part[:, i * size:(i + 1) * size] for part in images], axis=1) for i in range(4)], axis=0
    )
    result = lax.dot_general(
        joined,
        jnp.concatenate(weights, axis=1),
        (((1,), (1,)), ((), ())),
        preferred_element_type=jnp.float32,
    ).astype(BF16)
    for i in range(4):
        out_screened[i] = result[i * size:(i + 1) * size]
    last = pltpu.make_async_copy(out_screened, screened, out_sem.at[2])
    for copy in copies:
        copy.start()
    last.start()
    for copy in copies:
        copy.wait()
    last.wait()


def solution(mesh):
    n_energy, n_space = mesh.shape["energy"], mesh.shape["space"]

    def local(greens, coulomb, pattern):
        size = greens.shape[-1]
        rows = size // n_energy
        forward, inverse = make_tables(n_energy, rows)
        anywhere = pl.BlockSpec(memory_space=pl.ANY)
        vmem = pl.BlockSpec(memory_space=pltpu.VMEM)
        dma = pltpu.SemaphoreType.DMA
        strips = n_energy // 4
        polar = pl.pallas_call(
            lambda *refs: exchange_kernel(n_energy, n_space, rows, *refs),
            out_shape=pltpu.VMEM((3, 4, 2, size // 2, size), BF16),
            in_specs=[anywhere] * 3,
            out_specs=vmem,
            scratch_shapes=[
                pltpu.VMEM((4, 2, size, size), BF16),
                pltpu.VMEM((4, 2, size, size), BF16),
                pltpu.VMEM((strips, 4, 2, 4 * rows, size), BF16),
                pltpu.VMEM(forward.shape, BF16),
                pltpu.VMEM(inverse.shape, BF16),
                pltpu.VMEM((4, 2, size // 2, size), BF16),
                dma, dma, dma, dma((strips,)), dma, dma, dma, dma, dma, dma, dma((4,)),
                pltpu.SemaphoreType.REGULAR, pltpu.SemaphoreType.REGULAR,
            ],
            compiler_params=pltpu.CompilerParams(collective_id=0, has_side_effects=True),
            name="exchange",
        )(greens.reshape(4, 2, size // 2, size), jnp.asarray(forward), jnp.asarray(inverse))
        sides, screened = pl.pallas_call(
            lambda *refs: product_kernel(n_space, *refs),
            out_shape=(
                jax.ShapeDtypeStruct((2, 2, 2, size, size), BF16),
                jax.ShapeDtypeStruct((4, size, size), BF16),
            ),
            in_specs=[vmem, vmem, vmem],
            out_specs=(anywhere, anywhere),
            scratch_shapes=[
                pltpu.VMEM((2, 2, 2, size, size), BF16),
                pltpu.VMEM((4, size, size), BF16),
                dma((3,)),
            ],
            compiler_params=pltpu.CompilerParams(vmem_limit_bytes=16 << 20),
            name="products",
        )(polar, coulomb.reshape(3, size, size), pattern)
        return sides.reshape(2, 2, 2, 1, size, size), screened.reshape(2, 2, 1, size, size)

    return jax.shard_map(
        local,
        mesh=mesh,
        in_specs=(P(None, None, "energy", "space", None), P(None, "space", None), P("space", None)),
        out_specs=(P(None, None, None, "energy", "space", None), P(None, None, "energy", "space", None)),
        check_vma=False,
    )
```
